128 devices in a mesh: walker: 4 (over x), domain: 32 (over y, z, core).
Axes of the slice: x: 4, y: 4, z: 4, core: 2. Of those that a mesh axis runs over, the one named last changes fastest.
Arguments:
- positions: float32 [8, 3, 32768], P('walker', None, 'domain'), may hold values from -6 to 6
- velocities: float32 [8, 3, 32768], P('walker', None, 'domain'), may hold values from -6 to 6
- species: bfloat16 [32768, 128], P('domain'), may hold values from -6 to 6
- masses: float32 [32768], P('domain'), may hold values from 1 to 4
- send_rows: int32 [32768], P('domain'), may hold values from 0 to 1023
- neighbours: int32 [8, 8, 32768], P('walker', None, 'domain'), may hold values from 0 to 2047
- live_edges: int32 [8, 8, 32768], P('walker', None, 'domain'), may hold values 0 or 1
- w_rad: float32 [8, 128], replicated, may hold values from -2 to 2
- w_first: bfloat16 [128, 128], replicated, may hold values from -0.5 to 0.5
- w_second: bfloat16 [128, 128], replicated, may hold values from -0.5 to 0.5
- w_update: bfloat16 [128, 128], replicated, may hold values from -0.5 to 0.5
- w_out: float32 [128], replicated, may hold values from -0.5 to 0.5
- weights: float32 [8], replicated, may hold values from 0.1 to 1
- bins: int32 [8], replicated, may hold values from 0 to 3
- copy_src: int32 [8], replicated, may hold values from 0 to 7, as said below
Outputs:
- out_positions: float32 [8, 3, 32768], P('walker', None, 'domain')
- out_velocities: float32 [8, 3, 32768], P('walker', None, 'domain')
- new_weights: float32 [8], replicated
The draws below stay inside these ranges and needn't reach their ends.
Inputs may be any that keep to these rules, and one draw needn't show every extreme that they name: `copy_src`: every walker whose index is a multiple of 2, and the last walker, is copied into at least one slot.
All inputs are finite; a program needn't handle non-finite values. No bound on the sum of `live_edges` on one device may be relied on, other than what follows from the above.
Results may differ from the reference program's by a relative error of at most 0.0028.
Values may be sent and summed in bfloat16 or wider, within the bound.
A program may use at most 192 MiB of HBM per device.

```python
import math
import jax
import jax.numpy as jnp
from jax import lax

C = 128
NB = 8
NBR = 8
NBINS = 4
WALK_DEV = 2
ATOM_DEV = 1024
HALO = 512
WALKERS = 8
ATOMS = 32768
N_DOMAIN = 32


def draw_copy_src(key, part):
    merge_key = jax.random.fold_in(key, 11)
    target_key = jax.random.fold_in(key, 12)
    order_key = jax.random.fold_in(key, 13)
    walker_ids = jnp.arange(WALKERS).astype(jnp.int32)
    merged = jax.random.randint(merge_key, (WALKERS,), 0, 2)
    targets = jax.random.randint(target_key, (WALKERS,), 0, WALKERS).astype(jnp.int32)
    anchored = jnp.logical_or(walker_ids % WALK_DEV == 0, walker_ids == WALKERS - 1)
    keeping = jnp.logical_or(anchored, merged == 0)
    sources = jnp.where(keeping, walker_ids, targets)
    shuffled = jax.random.permutation(order_key, WALKERS)
    return sources[shuffled].astype(jnp.int32)


def place_ends(values, stream_key, least, high):
    place = [jax.random.randint(jax.random.fold_in(stream_key, axis), (), 0, length) for axis, length in enumerate(values.shape)]
    longest = values.shape.index(max(values.shape))
    next_to = place[:longest] + [(place[longest] + 1) % values.shape[longest]] + place[longest + 1:]
    return values.at[tuple(place)].set(least).at[tuple(next_to)].set(high)


def shard_levels(own_key, extent, shards, low, high):
    level, own = 1.0, jax.random.fold_in(own_key, 6)
    for dim, blocks in shards:
        heights = jnp.exp(jax.random.uniform(jax.random.fold_in(own, dim), (blocks,), jnp.float32, low / len(shards), high / len(shards)))
        level = level * jnp.repeat(heights, extent[dim] // blocks).reshape([-1 if axis == dim else 1 for axis in range(len(extent))])
    return level


def bell_draw(stream_key, dims, width, bound, shards=(), held_as=jnp.bfloat16):
    loudness = shard_levels(stream_key, dims, shards, -0.22, 0.18) if shards else 1.0
    entries = jax.random.normal(stream_key, dims, jnp.float32) * width * loudness
    return jnp.minimum(jnp.maximum(entries, -bound), bound).astype(held_as)


def setup_inputs(seed: int = 0) -> dict:
    key_of = jax.random.split(jax.random.key(seed), 16)
    return {
        "positions": bell_draw(key_of[0], (WALKERS, 3, ATOMS), 1.0, 6.0, ((0, 4), (2, 32)), jnp.float32),
        "velocities": bell_draw(key_of[1], (WALKERS, 3, ATOMS), 1.0, 6.0, ((0, 4), (2, 32)), jnp.float32),
        "species": bell_draw(key_of[2], (ATOMS, C), 1.0, 6.0, ((0, 32),)),
        "masses": jnp.clip(jnp.exp(math.log(4.0) - 1.3862944 * jax.random.uniform(key_of[3], (ATOMS,), jnp.float32) ** shard_levels(key_of[3], (ATOMS,), ((0, 32),), -0.2, 0.2)), 1.0, 4.0),
        "send_rows": place_ends(jax.random.randint(key_of[4], (2 * HALO * N_DOMAIN,), 0, ATOM_DEV), jax.random.fold_in(key_of[4], 1), 0, ATOM_DEV - 1).astype(jnp.int32),
        "neighbours": place_ends(jax.random.randint(key_of[5], (WALKERS, NBR, ATOMS), 0, ATOM_DEV + 2 * HALO), jax.random.fold_in(key_of[5], 1), 0, (ATOM_DEV + 2 * HALO) - 1).astype(jnp.int32),
        "live_edges": place_ends((jax.random.randint(key_of[6], (WALKERS, NBR, ATOMS), 0, 4) < 3).astype(jnp.int32), jax.random.fold_in(key_of[6], 1), 0, 1),
        "w_rad": bell_draw(key_of[7], (NB, C), NB ** -0.5, 2.0, (), jnp.float32),
        "w_first": bell_draw(key_of[8], (C, C), C ** -0.5, 0.5),
        "w_second": bell_draw(key_of[9], (C, C), C ** -0.5, 0.5),
        "w_update": bell_draw(key_of[10], (C, C), C ** -0.5, 0.5),
        "w_out": bell_draw(key_of[11], (C,), C ** -0.5, 0.5, (), jnp.float32),
        "weights": jnp.clip(jnp.exp(jax.random.uniform(key_of[12], (WALKERS,), jnp.float32, math.log(0.1), math.log(1.0))), 0.1, 1.0),
        "bins": place_ends(jax.random.randint(key_of[13], (WALKERS,), 0, NBINS), jax.random.fold_in(key_of[13], 1), 0, NBINS - 1).astype(jnp.int32),
        "copy_src": draw_copy_src(jax.random.fold_in(key_of[15], 71), 0),
    }


OFFSET = 2.0
CUTOFF = 5.0
STEP = 0.2

def edge_geometry(own_pos, ext_pos, nbr_index, w_rad):
    displace = ext_pos[:, nbr_index] - own_pos[:, None, :]
    distance = jnp.sqrt(lax.optimization_barrier(jnp.sum(displace * displace, axis=0)))
    scaled = distance / CUTOFF
    envelope = jnp.square(jnp.maximum(0.0, 1.0 - scaled * scaled))
    orders = jnp.arange(1, w_rad.shape[0] + 1).astype(jnp.float32)
    basis_vals = jnp.cos(scaled[..., None] * orders * math.pi) * envelope[..., None]
    hidden = jnp.einsum('sak,kc->sac', basis_vals, w_rad, precision=lax.Precision.HIGHEST)
    return (displace, jax.nn.silu(hidden).astype(jnp.bfloat16))

def reference(positions, velocities, species, masses, send_rows, neighbours, live_edges, w_rad, w_first, w_second, w_update, w_out, weights, bins, copy_src):
    num_domains = N_DOMAIN
    atom_count = ATOM_DEV
    halo_rows = HALO
    channels = species.shape[1]
    domains = jnp.arange(num_domains).astype(jnp.int32)[:, None]
    send_table = send_rows.reshape(num_domains, 2 * halo_rows)
    offset_vec = jnp.array([OFFSET, 0.0, 0.0], dtype=jnp.float32)[:, None, None]
    species_dom = species.reshape(num_domains, atom_count, channels)
    sent_species = species_dom[domains, send_table]
    species_ext = jnp.concatenate([species_dom, jnp.roll(sent_species[:, halo_rows:], 1, axis=0), jnp.roll(sent_species[:, :halo_rows], -1, axis=0)], axis=1)
    domain_list = jnp.arange(num_domains).astype(jnp.int32)

    def one_walker(inputs):
        pos_walker, vel_walker, nbr_walker, live_walker = inputs
        pos_dom = pos_walker.reshape(3, num_domains, atom_count)
        sent_pos = pos_dom[:, domains, send_table]
        pos_ext = jnp.concatenate([pos_dom, jnp.roll(sent_pos[..., halo_rows:], 1, axis=1) - offset_vec, jnp.roll(sent_pos[..., :halo_rows], -1, axis=1) + offset_vec], axis=2)
        nbr_dom = nbr_walker.reshape(-1, num_domains, atom_count)
        live_dom = live_walker.reshape(-1, num_domains, atom_count).astype(jnp.float32)

        def first_pass(index):
            nbr_index = nbr_dom[:, index]
            displace, hidden = edge_geometry(pos_dom[:, index], pos_ext[:, index], nbr_index, w_rad)
            filtered = jnp.einsum('sac,cd->sad', hidden.astype(jnp.float32), w_first.astype(jnp.float32))
            messages = filtered * species_ext[index][nbr_index].astype(jnp.float32) * live_dom[:, index][..., None]
            aggregate = lax.optimization_barrier(jnp.sum(messages, axis=0)).astype(jnp.bfloat16)
            updated = jnp.dot(aggregate, w_update, preferred_element_type=jnp.float32)
            return (species_dom[index].astype(jnp.float32) + jax.nn.silu(updated)).astype(jnp.bfloat16)
        features = lax.map(first_pass, domain_list)
        sent_feat = features[domains, send_table]
        feat_ext = jnp.concatenate([features, jnp.roll(sent_feat[:, halo_rows:], 1, axis=0), jnp.roll(sent_feat[:, :halo_rows], -1, axis=0)], axis=1)

        def second_pass(index):
            nbr_index = nbr_dom[:, index]
            displace, hidden = edge_geometry(pos_dom[:, index], pos_ext[:, index], nbr_index, w_rad)
            filtered = jnp.einsum('sac,cd->sad', hidden.astype(jnp.float32), w_second.astype(jnp.float32))
            coupling = lax.optimization_barrier(jnp.sum(filtered * w_out * features[index].astype(jnp.float32) * feat_ext[index][nbr_index].astype(jnp.float32), axis=-1)) * live_dom[:, index]
            pair_force = coupling[None] * displace
            reaction = jnp.zeros((3, atom_count + 2 * halo_rows), jnp.float32).at[:, nbr_index].add(-pair_force)
            return (lax.optimization_barrier(jnp.sum(pair_force, axis=1)) + reaction[:, :atom_count], reaction[:, atom_count:])
        own_force, halo_force = lax.map(second_pass, domain_list)
        returned = jnp.concatenate([jnp.roll(halo_force[..., halo_rows:], 1, axis=0), jnp.roll(halo_force[..., :halo_rows], -1, axis=0)], axis=-1)
        forces = jax.vmap(lambda force_row, table_row, back_row: force_row.at[:, table_row].add(back_row))(own_force, send_table, returned)
        forces = jnp.transpose(forces, (1, 0, 2)).reshape(3, num_domains * atom_count)
        vel_step = vel_walker + STEP * forces / masses
        pos_step = pos_walker + STEP * vel_step
        return (pos_step, vel_step)
    pos_step, vel_step = lax.map(one_walker, (positions, velocities, neighbours, live_edges))
    src_weight = weights[copy_src]
    src_bin = bins[copy_src]
    same_bin = (src_bin[:, None] == src_bin[None, :]).astype(jnp.float32)
    bin_share = lax.optimization_barrier(jnp.sum(same_bin * src_weight[None, :], axis=1))
    bin_mass = lax.optimization_barrier(jnp.sum((src_bin[:, None] == bins[None, :]).astype(jnp.float32) * weights[None, :], axis=1))
    new_weights = bin_mass * src_weight / bin_share
    return (pos_step[copy_src], vel_step[copy_src], new_weights)
```

```python
import functools
import math

import jax
import jax.numpy as jnp
from jax import lax
from jax.experimental import pallas as pl
from jax.experimental.pallas import tpu as pltpu
from jax.sharding import PartitionSpec as P

OFFSET = 2.0
CUTOFF = 5.0
STEP = 0.2
LANES = 128
MESH = pl.DeviceIdType.MESH
F32 = jnp.float32
BF16 = jnp.bfloat16


def lane_iota(shape):
    return lax.broadcasted_iota(jnp.int32, shape, len(shape) - 1)


def row_iota(shape):
    return lax.broadcasted_iota(jnp.int32, shape, 0)


def one_hot(column, width):
    rows = column.shape[0]
    wide = jnp.broadcast_to(column, (rows, LANES))
    lanes = lane_iota((rows, LANES))
    return jnp.concatenate(
        [(wide == lanes + j * LANES).astype(F32).astype(BF16) for j in range(width // LANES)], axis=1
    )


def silu(x):
    half = 0.5 * x
    return half + half * jnp.tanh(half)


def split(x):
    head = x.astype(BF16).astype(F32)
    return head, x - head


def dot(a, b):
    return jnp.dot(a, b, preferred_element_type=F32)


def lane_lookup(rows, hi, lo):
    found = jnp.zeros(lo.shape, F32)
    for r, row in enumerate(rows):
        picked = jnp.take_along_axis(
            jnp.broadcast_to(row, lo.shape), lo, axis=1, mode="promise_in_bounds"
        )
        found = jnp.where(hi == r, picked, found)
    return found


def kernel(
    pos, vel, spc, mas, send, nbr, liv, wrad, w1, w2, wup, wout, wts, bns, csr, csr_s,
    opos, ovel, onw,
    send_pos, halo_pos, send_spc, halo_spc, feat, send_feat, halo_feat, filt2, oh, send_oh,
    send_lo, gath, disp, wbig, sumw, wcat, acc, force, send_frc, recv_frc, every, prod,
    send_sem, recv_sem,
):
    n_walk, n_dom = lax.axis_size("walker"), lax.axis_size("domain")
    me_w, me_d = lax.axis_index("walker"), lax.axis_index("domain")
    left = lax.rem(me_d + n_dom - 1, n_dom)
    right = lax.rem(me_d + 1, n_dom)
    walkers, atoms = pos.shape[0], pos.shape[2]
    halo = send.shape[1] // 2
    groups = atoms // LANES
    slots = nbr.shape[1]
    tile_edges = slots * LANES
    peers = [(me_w, left), (me_w, right)]
    peers += [(lax.rem(me_w + o, n_walk), me_d) for o in range(1, n_walk)]

    barrier = pltpu.get_barrier_semaphore()
    for peer in peers:
        pl.semaphore_signal(barrier, inc=1, device_id=peer, device_id_type=MESH)

    def remote(src, dst, sem, peer):
        return pltpu.make_async_remote_copy(
            src_ref=src,
            dst_ref=dst,
            send_sem=send_sem.at[sem],
            recv_sem=recv_sem.at[sem],
            device_id=peer,
            device_id_type=MESH,
        )

    def both_ways(src, dst, sem):
        copies = [
            remote(src.at[0], dst.at[1], sem, peers[0]),
            remote(src.at[1], dst.at[0], sem + 1, peers[1]),
        ]
        for copy in copies:
            copy.start()
        return copies

    rows_out = jnp.concatenate(
        [send[:, g * LANES : (g + 1) * LANES] for g in range(groups)], axis=0
    )
    out_hi, out_lo = rows_out >> 7, rows_out & (LANES - 1)
    per_side = groups // 2
    for w in range(walkers):
        for c in range(3):
            table = [pos[w, c : c + 1, r * LANES : (r + 1) * LANES] for r in range(groups)]
            sent = lane_lookup(table, out_hi, out_lo)
            row = w * 3 + c
            for g in range(groups):
                q = g % per_side
                send_pos[g // per_side, row : row + 1, q * LANES : (q + 1) * LANES] = sent[g : g + 1]
    columns_out = jnp.transpose(rows_out)
    lo_out = jnp.transpose(out_lo)
    for g in range(groups):
        block = slice(g * LANES, (g + 1) * LANES)
        send_oh[block, :] = one_hot(columns_out[:, g : g + 1], atoms)
        send_lo[block, :] = one_hot(lo_out[:, g : g + 1], LANES)
    pl.semaphore_wait(barrier, len(peers))
    moves = both_ways(send_pos, halo_pos, 0)
    sent = dot(send_oh[...], spc[...]).astype(BF16)
    send_spc[0] = sent[:halo]
    send_spc[1] = sent[halo:]
    moves += both_ways(send_spc, halo_spc, 2)

    def weights_by_slot():
        heads, tails = split(wrad[...])
        sub = row_iota((slots, LANES))
        for s in range(slots):
            blocks = []
            for piece in (heads, tails):
                for _ in range(2):
                    for k in range(piece.shape[0]):
                        line = jnp.broadcast_to(piece[k : k + 1, :], (slots, LANES))
                        blocks.append(jnp.where(sub == s, line, 0.0))
            wbig[:, s * LANES : (s + 1) * LANES] = jnp.concatenate(blocks, axis=0).astype(BF16)

    weights_by_slot()
    for s in range(slots):
        sumw[s * 2 * LANES : (s + 1) * 2 * LANES, :] = (
            (lane_iota((2 * LANES, LANES)) == s).astype(F32).astype(BF16)
        )
    wcat[:, :LANES] = w1[...]
    wcat[:, LANES:] = w2[...]

    count = wts.shape[1]
    square = (count, count)
    eye = (lane_iota(square) == row_iota(square)).astype(F32)

    def to_column(row):
        return jnp.sum(eye * row, axis=1, keepdims=True)

    def to_row(column):
        return jnp.sum(eye * column, axis=0, keepdims=True)

    w_row, b_row = wts[...], bns[...].astype(F32)
    chosen = (to_column(csr[...].astype(F32)) == lane_iota(square).astype(F32)).astype(F32)
    src_w = jnp.sum(chosen * w_row, axis=1, keepdims=True)
    src_b = jnp.sum(chosen * b_row, axis=1, keepdims=True)
    mass = jnp.sum((src_b == b_row).astype(F32) * w_row, axis=1, keepdims=True)
    share = jnp.sum((src_b == to_row(src_b)).astype(F32) * to_row(src_w), axis=1, keepdims=True)
    onw[...] = to_row(mass * src_w / share)

    for copy in moves:
        copy.wait()

    def edge_ids(w, at):
        ids = nbr[w, :, at]
        key = (ids >> 10) * halo + (ids & (halo - 1))
        key = jnp.where(liv[w, :, at] != 0, key, -1)
        return ids, key, (ids >> 9) & 1

    def gather_rows(key, second, own, near):
        key_t = jnp.transpose(key)
        second_t = jnp.transpose(second)
        for s in range(slots):
            oh[s * LANES : (s + 1) * LANES, :] = one_hot(key_t[:, s : s + 1], 2 * halo)
        table = jnp.concatenate(
            [
                jnp.concatenate([own[:halo], own[halo:]], axis=1),
                jnp.concatenate([near[0], near[1]], axis=1),
            ],
            axis=0,
        )
        both = dot(oh[...], table)
        for s in range(slots):
            block = slice(s * LANES, (s + 1) * LANES)
            take = jnp.broadcast_to(second_t[:, s : s + 1], (LANES, LANES)) != 0
            gath[block, :] = jnp.where(take, both[block, LANES:], both[block, :LANES])

    def geometry(w, at, ids):
        hi, lo = ids >> 7, ids & (LANES - 1)
        square_sum = None
        for c in range(3):
            table = [pos[w, c : c + 1, r * LANES : (r + 1) * LANES] for r in range(groups)]
            for side in range(2):
                shift = 0.0 if c else (OFFSET if side else -OFFSET)
                for q in range(per_side):
                    row = w * 3 + c
                    table.append(
                        halo_pos[side, row : row + 1, q * LANES : (q + 1) * LANES] + shift
                    )
            delta = lane_lookup(table, hi, lo) - pos[w, c : c + 1, at]
            disp[w, c, :, at] = delta
            square_sum = delta * delta if c == 0 else square_sum + delta * delta
        scaled = jnp.sqrt(square_sum) / CUTOFF
        envelope = jnp.square(jnp.maximum(0.0, 1.0 - scaled * scaled))
        first = jnp.cos(jnp.minimum(scaled, 1.0) * math.pi)
        waves = [first, 2.0 * first * first - 1.0]
        while len(waves) < wrad.shape[0]:
            waves.append(2.0 * first * waves[-1] - waves[-2])
        pieces = [split(wave * envelope) for wave in waves]
        stacked = jnp.concatenate([p[0] for p in pieces] + [p[1] for p in pieces], axis=0)
        turned = jnp.transpose(stacked).astype(BF16)
        return jnp.concatenate([turned, turned], axis=1)

    def first_pass(w, t):
        at = pl.ds(pl.multiple_of(t * LANES, LANES), LANES)
        ids, key, second = edge_ids(w, at)
        basis = geometry(w, at, ids)
        gather_rows(key, second, spc[...], halo_spc)
        total = jnp.zeros((LANES, LANES), F32)
        for s in range(0, slots, 2):
            hidden = dot(basis, wbig[:, s * LANES : (s + 2) * LANES])
            radial = silu(hidden).astype(BF16)
            for i in range(2):
                block = slice((s + i) * LANES, (s + i + 1) * LANES)
                filters = dot(radial[:, i * LANES : (i + 1) * LANES], wcat[...])
                filt2[w, t, block, :] = filters[:, LANES:]
                total = total + filters[:, :LANES] * gath[block, :]
        updated = dot(total.astype(BF16), wup[...])
        feat[w, at, :] = (spc[at, :].astype(F32) + silu(updated)).astype(BF16)

    def second_pass(w, t):
        at = pl.ds(pl.multiple_of(t * LANES, LANES), LANES)
        ids, key, second = edge_ids(w, at)
        gather_rows(key, second, feat[w], halo_feat[w])
        own = feat[w, at, :].astype(F32) * wout[...]
        for s in range(slots):
            block = slice(s * LANES, (s + 1) * LANES)
            head, tail = split(filt2[w, t, block, :] * own * gath[block, :])
            prod[:, 2 * s * LANES : (2 * s + 1) * LANES] = head.astype(BF16)
            prod[:, (2 * s + 1) * LANES : (2 * s + 2) * LANES] = tail.astype(BF16)
        coupling = jnp.transpose(dot(prod[...], sumw[...]))[:slots]
        hi, lo = ids >> 7, ids & (LANES - 1)
        pieces = []
        for c in range(3):
            pair = coupling * disp[w, c, :, at]
            force[w, c, pl.ds(t, 1), :] = jnp.sum(pair, axis=0, keepdims=True)
            pieces.append(split(pair))
        acc[...] += spread(pieces, hi, lo, 2 * groups)

    def spread_left(pieces, hi, high_count):
        sub = row_iota((high_count, LANES))
        out = []
        for s in range(hi.shape[0]):
            here = jnp.broadcast_to(hi[s : s + 1], (high_count, LANES)) == sub
            rows = [
                jnp.where(here, jnp.broadcast_to(x[p][s : s + 1], (high_count, LANES)), 0.0)
                for p in range(2)
                for x in pieces
            ]
            out.append(jnp.concatenate(rows, axis=0).astype(BF16))
        return jnp.concatenate(out, axis=1)

    def spread(pieces, hi, lo, high_count):
        lo_t = jnp.transpose(lo)
        low = jnp.concatenate([one_hot(lo_t[:, s : s + 1], LANES) for s in range(slots)], axis=0)
        return dot(spread_left(pieces, hi, high_count), low)

    def loop(body, w):
        def step(t, carry):
            body(w, t)
            return carry

        lax.fori_loop(0, groups, step, 0)

    feat_moves = []
    for w in range(walkers):
        loop(first_pass, w)
        sent = dot(send_oh[...], feat[w]).astype(BF16)
        send_feat[w, 0] = sent[:halo]
        send_feat[w, 1] = sent[halo:]
        feat_moves.append(both_ways(send_feat.at[w], halo_feat.at[w], 4 + 2 * w))

    force_moves = []
    high = 2 * groups
    for w in range(walkers):
        for copy in feat_moves[w]:
            copy.wait()
        acc[...] = jnp.zeros_like(acc)
        loop(second_pass, w)
        reaction = acc[: 3 * high] + acc[3 * high :]
        for c in range(3):
            force[w, c] = force[w, c] - reaction[c * high : c * high + groups]
            for side in range(2):
                start = c * high + groups + side * per_side
                send_frc[w, side, c * per_side : (c + 1) * per_side, :] = -reaction[
                    start : start + per_side
                ]
        base = 4 + 2 * walkers + 2 * w
        force_moves.append(both_ways(send_frc.at[w], recv_frc.at[w], base))

    state_moves = []
    for w in range(walkers):
        for copy in force_moves[w]:
            copy.wait()
        pieces = []
        for c in range(3):
            rows = slice(c * per_side, (c + 1) * per_side)
            pieces.append(
                split(jnp.concatenate([recv_frc[w, 0, rows, :], recv_frc[w, 1, rows, :]], axis=0))
            )
        back = dot(spread_left(pieces, out_hi, groups), send_lo[...])
        for c in range(3):
            total = force[w, c] + (
                back[c * groups : (c + 1) * groups]
                + back[(3 + c) * groups : (4 + c) * groups]
            )
            flat = jnp.concatenate([total[g : g + 1] for g in range(groups)], axis=1)
            stepped = vel[w, c : c + 1, :] + STEP * flat / mas[...]
            every[w, c : c + 1, :] = pos[w, c : c + 1, :] + STEP * stepped
            every[w, 3 + c : 4 + c, :] = stepped
        for o in range(1, n_walk):
            base = 4 + 4 * walkers + w * (n_walk - 1) + o - 1
            copy = remote(every.at[w], every.at[o * walkers + w], base, peers[1 + o])
            copy.start()
            state_moves.append(copy)
    for copy in state_moves:
        copy.wait()
    for k in range(walkers):
        source = csr_s[me_w * walkers + k]
        behind = lax.rem(me_w - lax.div(source, walkers) + n_walk, n_walk)
        picked = every[behind * walkers + lax.rem(source, walkers)]
        opos[k] = picked[:3]
        ovel[k] = picked[3:6]


def on_device(
    positions,
    velocities,
    species,
    masses,
    send_rows,
    neighbours,
    live_edges,
    w_rad,
    w_first,
    w_second,
    w_update,
    w_out,
    weights,
    bins,
    copy_src,
):
    walkers, _, atoms = positions.shape
    channels = species.shape[1]
    halo = send_rows.shape[0] // 2
    groups = atoms // LANES
    slots = neighbours.shape[1]
    orders = w_rad.shape[0]
    n_walk = lax.axis_size("walker")
    edges = slots * LANES
    copies = 4 + 4 * walkers + walkers * (n_walk - 1)
    vmem = pl.BlockSpec(memory_space=pltpu.VMEM)
    smem = pl.BlockSpec(memory_space=pltpu.SMEM)
    halo_rows = (2, halo, channels)
    out_positions, out_velocities, new_weights = pl.pallas_call(
        kernel,
        out_shape=(
            jax.ShapeDtypeStruct(positions.shape, F32),
            jax.ShapeDtypeStruct(velocities.shape, F32),
            jax.ShapeDtypeStruct((1, weights.shape[0]), F32),
        ),
        in_specs=[vmem] * 15 + [smem],
        out_specs=(vmem, vmem, vmem),
        scratch_shapes=[
            pltpu.VMEM((2, 8, halo), F32),
            pltpu.VMEM((2, 8, halo), F32),
            pltpu.VMEM(halo_rows, BF16),
            pltpu.VMEM(halo_rows, BF16),
            pltpu.VMEM((walkers, atoms, channels), BF16),
            pltpu.VMEM((walkers, *halo_rows), BF16),
            pltpu.VMEM((walkers, *halo_rows), BF16),
            pltpu.VMEM((walkers, groups, edges, channels), F32),
            pltpu.VMEM((edges, 2 * halo), BF16),
            pltpu.VMEM((2 * halo, atoms), BF16),
            pltpu.VMEM((2 * halo, LANES), BF16),
            pltpu.VMEM((edges, channels), F32),
            pltpu.VMEM((walkers, 3, slots, atoms), F32),
            pltpu.VMEM((4 * orders * slots, slots * channels), BF16),
            pltpu.VMEM((slots * 2 * channels, LANES), BF16),
            pltpu.VMEM((channels, 2 * channels), BF16),
            pltpu.VMEM((12 * groups, LANES), F32),
            pltpu.VMEM((walkers, 3, groups, LANES), F32),
            pltpu.VMEM((walkers, 2, 16, LANES), F32),
            pltpu.VMEM((walkers, 2, 16, LANES), F32),
            pltpu.VMEM((n_walk * walkers, 8, atoms), F32),
            pltpu.VMEM((LANES, slots * 2 * channels), BF16),
            pltpu.SemaphoreType.DMA((copies,)),
            pltpu.SemaphoreType.DMA((copies,)),
        ],
        compiler_params=pltpu.CompilerParams(
            collective_id=0, has_side_effects=True, vmem_limit_bytes=48 * 2**20
        ),
    )(
        positions,
        velocities,
        species,
        masses[None],
        send_rows[None],
        neighbours,
        live_edges,
        w_rad,
        w_first,
        w_second,
        w_update,
        w_out[None],
        weights[None],
        bins[None],
        copy_src[None],
        copy_src,
    )
    return out_positions, out_velocities, new_weights[0]


def solution(mesh):
    in_specs = (
        P("walker", None, "domain"),
        P("walker", None, "domain"),
        P("domain", None),
        P("domain"),
        P("domain"),
        P("walker", None, "domain"),
        P("walker", None, "domain"),
        P(),
        P(),
        P(),
        P(),
        P(),
        P(),
        P(),
        P(),
    )
    out_specs = (P("walker", None, "domain"), P("walker", None, "domain"), P())
    return jax.shard_map(
        on_device, mesh=mesh, in_specs=in_specs, out_specs=out_specs, check_vma=False
    )
```

```python
import functools
import math

import jax
import jax.numpy as jnp
from jax import lax
from jax.experimental import pallas as pl
from jax.experimental.pallas import tpu as pltpu
from jax.sharding import PartitionSpec as P

OFFSET = 2.0
CUTOFF = 5.0
STEP = 0.2
LANES = 128
MESH = pl.DeviceIdType.MESH
F32 = jnp.float32
BF16 = jnp.bfloat16


def lane_iota(shape):
    return lax.broadcasted_iota(jnp.int32, shape, len(shape) - 1)


def row_iota(shape):
    return lax.broadcasted_iota(jnp.int32, shape, 0)


def one_hot(column, width):
    rows = column.shape[0]
    wide = jnp.broadcast_to(column, (rows, LANES)).astype(jnp.int16)
    lanes = lane_iota((rows, LANES))
    one, zero = jnp.ones((rows, LANES), BF16), jnp.zeros((rows, LANES), BF16)
    return jnp.concatenate(
        [
            jnp.where(wide == (lanes + j * LANES).astype(jnp.int16), one, zero)
            for j in range(width // LANES)
        ],
        axis=1,
    )


def silu(x):
    half = 0.5 * x
    return half + half * jnp.tanh(half)


def split(x):
    head = x.astype(BF16).astype(F32)
    return head, x - head


def dot(a, b):
    return jnp.dot(a, b, preferred_element_type=F32)


def lane_lookup(rows, hi, lo):
    found = jnp.zeros(lo.shape, F32)
    for r, row in enumerate(rows):
        picked = jnp.take_along_axis(
            jnp.broadcast_to(row, lo.shape), lo, axis=1, mode="promise_in_bounds"
        )
        found = jnp.where(hi == r, picked, found)
    return found


def kernel(
    pos_h, vel_h, spc_h, mas_h, send_h, nbr_h, liv_h, wrad_h, w1_h, w2_h, wup_h, wout_h,
    wts, bns, csr, csr_s,
    opos, ovel, onw,
    pos, vel, spc, mas, send, nbr, liv, wrad, w1, w2, wup, wout,
    send_pos, halo_pos, send_spc, halo_spc, feat, send_feat, halo_feat, filt2, oh, send_oh,
    send_lo, low, gath, disp, wbig, sumw, wcat, acc, force, send_frc, recv_frc, every, prod,
    load_sem, send_sem, recv_sem,
):
    n_walk, n_dom = lax.axis_size("walker"), lax.axis_size("domain")
    me_w, me_d = lax.axis_index("walker"), lax.axis_index("domain")
    left = lax.rem(me_d + n_dom - 1, n_dom)
    right = lax.rem(me_d + 1, n_dom)
    walkers, atoms = pos.shape[1], pos.shape[2]
    halo = send.shape[1] // 2
    groups = atoms // LANES
    slots = nbr.shape[1]
    tile_edges = slots * LANES
    peers = [(me_w, left), (me_w, right)]
    peers += [(lax.rem(me_w + o, n_walk), me_d) for o in range(1, n_walk)]

    barrier = pltpu.get_barrier_semaphore()
    for peer in peers:
        pl.semaphore_signal(barrier, inc=1, device_id=peer, device_id_type=MESH)

    loads = {}
    for i, (name, src, dst) in enumerate(
        [
            ("send", send_h, send),
            ("pos", pos_h, pos),
            ("spc", spc_h, spc),
            ("nbr", nbr_h, nbr),
            ("liv", liv_h, liv),
            ("wrad", wrad_h, wrad),
            ("w1", w1_h, w1),
            ("w2", w2_h, w2),
            ("wup", wup_h, wup),
            ("wout", wout_h, wout),
            ("vel", vel_h, vel),
            ("mas", mas_h, mas),
        ]
    ):
        loads[name] = pltpu.make_async_copy(src, dst, load_sem.at[i])
        loads[name].start()

    def remote(src, dst, sem, peer):
        return pltpu.make_async_remote_copy(
            src_ref=src,
            dst_ref=dst,
            send_sem=send_sem.at[sem],
            recv_sem=recv_sem.at[sem],
            device_id=peer,
            device_id_type=MESH,
        )

    def both_ways(src, dst, sem):
        copies = [
            remote(src.at[0], dst.at[1], sem, peers[0]),
            remote(src.at[1], dst.at[0], sem + 1, peers[1]),
        ]
        for copy in copies:
            copy.start()
        return copies

    loads["send"].wait()
    loads["pos"].wait()
    rows_out = jnp.concatenate(
        [send[:, g * LANES : (g + 1) * LANES] for g in range(groups)], axis=0
    )
    out_hi, out_lo = rows_out >> 7, rows_out & (LANES - 1)
    per_side = groups // 2
    for w in range(walkers):
        for c in range(3):
            table = [pos[c, w : w + 1, r * LANES : (r + 1) * LANES] for r in range(groups)]
            sent = lane_lookup(table, out_hi, out_lo)
            row = w * 3 + c
            for g in range(groups):
                q = g % per_side
                send_pos[g // per_side, row : row + 1, q * LANES : (q + 1) * LANES] = sent[g : g + 1]
    columns_out = jnp.transpose(rows_out)
    lo_out = jnp.transpose(out_lo)
    for g in range(groups):
        block = slice(g * LANES, (g + 1) * LANES)
        send_oh[block, :] = one_hot(columns_out[:, g : g + 1], atoms)
        send_lo[block, :] = one_hot(lo_out[:, g : g + 1], LANES)
    loads["spc"].wait()
    pl.semaphore_wait(barrier, len(peers))
    moves = both_ways(send_pos, halo_pos, 0)
    sent = dot(send_oh[...], spc[...]).astype(BF16)
    send_spc[0] = sent[:halo]
    send_spc[1] = sent[halo:]
    moves += both_ways(send_spc, halo_spc, 2)

    for name in ("nbr", "liv", "wrad", "w1", "w2", "wup", "wout", "vel", "mas"):
        loads[name].wait()

    def weights_by_slot():
        heads, tails = split(wrad[...])
        sub = row_iota((slots, LANES))
        for s in range(slots):
            blocks = []
            for piece in (heads, tails):
                for _ in range(2):
                    for k in range(piece.shape[0]):
                        line = jnp.broadcast_to(piece[k : k + 1, :], (slots, LANES))
                        blocks.append(jnp.where(sub == s, line, 0.0))
            wbig[:, s * LANES : (s + 1) * LANES] = jnp.concatenate(blocks, axis=0).astype(BF16)

    weights_by_slot()
    for s in range(slots):
        sumw[s * 2 * LANES : (s + 1) * 2 * LANES, :] = (
            (lane_iota((2 * LANES, LANES)) == s).astype(F32).astype(BF16)
        )
    wcat[:, :LANES] = w1[...]
    wcat[:, LANES:] = w2[...]

    count = wts.shape[1]
    square = (count, count)
    eye = (lane_iota(square) == row_iota(square)).astype(F32)

    def to_column(row):
        return jnp.sum(eye * row, axis=1, keepdims=True)

    def to_row(column):
        return jnp.sum(eye * column, axis=0, keepdims=True)

    w_row, b_row = wts[...], bns[...].astype(F32)
    chosen = (to_column(csr[...].astype(F32)) == lane_iota(square).astype(F32)).astype(F32)
    src_w = jnp.sum(chosen * w_row, axis=1, keepdims=True)
    src_b = jnp.sum(chosen * b_row, axis=1, keepdims=True)
    mass = jnp.sum((src_b == b_row).astype(F32) * w_row, axis=1, keepdims=True)
    share = jnp.sum((src_b == to_row(src_b)).astype(F32) * to_row(src_w), axis=1, keepdims=True)
    onw[...] = to_row(mass * src_w / share)

    def build(w, t):
        at = pl.ds(pl.multiple_of(t * LANES, LANES), LANES)
        ids = nbr[w, :, at]
        key = (ids >> 10) * halo + (ids & (halo - 1))
        key_t = jnp.transpose(jnp.where(liv[w, :, at] != 0, key, -1))
        lo_t = jnp.transpose(ids & (LANES - 1))
        for s in range(slots):
            block = slice(s * LANES, (s + 1) * LANES)
            oh[w, t, block, :] = one_hot(key_t[:, s : s + 1], 2 * halo)
            low[w, t, block, :] = one_hot(lo_t[:, s : s + 1], LANES)

    def gather_rows(w, t, ids, own, near):
        second_t = jnp.transpose((ids >> 9) & 1)
        table = jnp.concatenate(
            [
                jnp.concatenate([own[:halo], own[halo:]], axis=1),
                jnp.concatenate([near[0], near[1]], axis=1),
            ],
            axis=0,
        )
        both = dot(oh[w, t], table)
        for s in range(slots):
            block = slice(s * LANES, (s + 1) * LANES)
            take = jnp.broadcast_to(second_t[:, s : s + 1], (LANES, LANES)) != 0
            gath[block, :] = jnp.where(take, both[block, LANES:], both[block, :LANES])

    def geometry(w, at, ids):
        hi, lo = ids >> 7, ids & (LANES - 1)
        square_sum = None
        for c in range(3):
            table = [pos[c, w : w + 1, r * LANES : (r + 1) * LANES] for r in range(groups)]
            for side in range(2):
                shift = 0.0 if c else (OFFSET if side else -OFFSET)
                for q in range(per_side):
                    row = w * 3 + c
                    table.append(
                        halo_pos[side, row : row + 1, q * LANES : (q + 1) * LANES] + shift
                    )
            delta = lane_lookup(table, hi, lo) - pos[c, w : w + 1, at]
            disp[w, c, :, at] = delta
            square_sum = delta * delta if c == 0 else square_sum + delta * delta
        scaled = jnp.sqrt(square_sum) / CUTOFF
        envelope = jnp.square(jnp.maximum(0.0, 1.0 - scaled * scaled))
        first = jnp.cos(jnp.minimum(scaled, 1.0) * math.pi)
        waves = [first, 2.0 * first * first - 1.0]
        while len(waves) < wrad.shape[0]:
            waves.append(2.0 * first * waves[-1] - waves[-2])
        pieces = [split(wave * envelope) for wave in waves]
        stacked = jnp.concatenate([p[0] for p in pieces] + [p[1] for p in pieces], axis=0)
        turned = jnp.transpose(stacked).astype(BF16)
        return jnp.concatenate([turned, turned], axis=1)

    def first_pass(w, t):
        at = pl.ds(pl.multiple_of(t * LANES, LANES), LANES)
        ids = nbr[w, :, at]
        basis = geometry(w, at, ids)
        gather_rows(w, t, ids, spc[...], halo_spc)
        total = jnp.zeros((LANES, LANES), F32)
        for s in range(0, slots, 2):
            hidden = dot(basis, wbig[:, s * LANES : (s + 2) * LANES])
            radial = silu(hidden).astype(BF16)
            for i in range(2):
                block = slice((s + i) * LANES, (s + i + 1) * LANES)
                filters = dot(radial[:, i * LANES : (i + 1) * LANES], wcat[...])
                filt2[w, t, block, :] = filters[:, LANES:]
                total = total + filters[:, :LANES] * gath[block, :]
        updated = dot(total.astype(BF16), wup[...])
        feat[w, at, :] = (spc[at, :].astype(F32) + silu(updated)).astype(BF16)

    def second_pass(w, t):
        at = pl.ds(pl.multiple_of(t * LANES, LANES), LANES)
        ids = nbr[w, :, at]
        gather_rows(w, t, ids, feat[w], halo_feat[w])
        own = feat[w, at, :].astype(F32) * wout[...]
        for s in range(slots):
            block = slice(s * LANES, (s + 1) * LANES)
            head, tail = split(filt2[w, t, block, :] * own * gath[block, :])
            prod[:, 2 * s * LANES : (2 * s + 1) * LANES] = head.astype(BF16)
            prod[:, (2 * s + 1) * LANES : (2 * s + 2) * LANES] = tail.astype(BF16)
        coupling = jnp.transpose(dot(prod[...], sumw[...]))[:slots]
        hi = ids >> 7
        pieces = []
        for c in range(3):
            pair = coupling * disp[w, c, :, at]
            force[w, c, pl.ds(t, 1), :] = jnp.sum(pair, axis=0, keepdims=True)
            pieces.append(split(pair))
        acc[...] += dot(spread_left(pieces, hi, 2 * groups), low[w, t])

    def spread_left(pieces, hi, high_count):
        sub = row_iota((high_count, LANES))
        out = []
        for s in range(hi.shape[0]):
            here = jnp.broadcast_to(hi[s : s + 1], (high_count, LANES)) == sub
            rows = [
                jnp.where(here, jnp.broadcast_to(x[p][s : s + 1], (high_count, LANES)), 0.0)
                for p in range(2)
                for x in pieces
            ]
            out.append(jnp.concatenate(rows, axis=0).astype(BF16))
        return jnp.concatenate(out, axis=1)

    def loop(body, w):
        def step(t, carry):
            body(w, t)
            return carry

        lax.fori_loop(0, groups, step, 0)

    loop(build, 0)
    for copy in moves:
        copy.wait()
    feat_moves = []
    for w in range(walkers):
        if w:
            loop(build, w)
        loop(first_pass, w)
        sent = dot(send_oh[...], feat[w]).astype(BF16)
        send_feat[w, 0] = sent[:halo]
        send_feat[w, 1] = sent[halo:]
        feat_moves.append(both_ways(send_feat.at[w], halo_feat.at[w], 4 + 2 * w))

    force_moves = []
    high = 2 * groups
    for w in range(walkers):
        for copy in feat_moves[w]:
            copy.wait()
        acc[...] = jnp.zeros_like(acc)
        loop(second_pass, w)
        reaction = acc[: 3 * high] + acc[3 * high :]
        for c in range(3):
            force[w, c] = force[w, c] - reaction[c * high : c * high + groups]
            for side in range(2):
                start = c * high + groups + side * per_side
                send_frc[w, side, c * per_side : (c + 1) * per_side, :] = -reaction[
                    start : start + per_side
                ]
        base = 4 + 2 * walkers + 2 * w
        force_moves.append(both_ways(send_frc.at[w], recv_frc.at[w], base))

    state_moves = []
    for w in range(walkers):
        for copy in force_moves[w]:
            copy.wait()
        pieces = []
        for c in range(3):
            rows = slice(c * per_side, (c + 1) * per_side)
            pieces.append(
                split(jnp.concatenate([recv_frc[w, 0, rows, :], recv_frc[w, 1, rows, :]], axis=0))
            )
        back = dot(spread_left(pieces, out_hi, groups), send_lo[...])
        for c in range(3):
            total = force[w, c] + (
                back[c * groups : (c + 1) * groups]
                + back[(3 + c) * groups : (4 + c) * groups]
            )
            flat = jnp.concatenate([total[g : g + 1] for g in range(groups)], axis=1)
            stepped = vel[c, w : w + 1, :] + STEP * flat / mas[...]
            every[w, c : c + 1, :] = pos[c, w : w + 1, :] + STEP * stepped
            every[w, 3 + c : 4 + c, :] = stepped
        for o in range(1, n_walk):
            base = 4 + 4 * walkers + w * (n_walk - 1) + o - 1
            copy = remote(every.at[w], every.at[o * walkers + w], base, peers[1 + o])
            copy.start()
            state_moves.append(copy)
    for copy in state_moves:
        copy.wait()
    for k in range(walkers):
        source = csr_s[me_w * walkers + k]
        behind = lax.rem(me_w - lax.div(source, walkers) + n_walk, n_walk)
        picked = every[behind * walkers + lax.rem(source, walkers)]
        for c in range(3):
            opos[c, k : k + 1, :] = picked[c : c + 1]
            ovel[c, k : k + 1, :] = picked[3 + c : 4 + c]


def on_device(
    positions,
    velocities,
    species,
    masses,
    send_rows,
    neighbours,
    live_edges,
    w_rad,
    w_first,
    w_second,
    w_update,
    w_out,
    weights,
    bins,
    copy_src,
):
    walkers, _, atoms = positions.shape
    channels = species.shape[1]
    halo = send_rows.shape[0] // 2
    groups = atoms // LANES
    slots = neighbours.shape[1]
    orders = w_rad.shape[0]
    n_walk = lax.axis_size("walker")
    edges = slots * LANES
    copies = 4 + 4 * walkers + walkers * (n_walk - 1)
    by_component = (3, walkers, atoms)
    hbm = pl.BlockSpec(memory_space=pltpu.HBM)
    vmem = pl.BlockSpec(memory_space=pltpu.VMEM)
    smem = pl.BlockSpec(memory_space=pltpu.SMEM)
    halo_rows = (2, halo, channels)
    out_positions, out_velocities, new_weights = pl.pallas_call(
        kernel,
        out_shape=(
            jax.ShapeDtypeStruct(by_component, F32),
            jax.ShapeDtypeStruct(by_component, F32),
            jax.ShapeDtypeStruct((1, weights.shape[0]), F32),
        ),
        in_specs=[hbm] * 12 + [vmem] * 3 + [smem],
        out_specs=(vmem, vmem, vmem),
        scratch_shapes=[
            pltpu.VMEM(by_component, F32),
            pltpu.VMEM(by_component, F32),
            pltpu.VMEM(species.shape, BF16),
            pltpu.VMEM((1, atoms), F32),
            pltpu.VMEM((1, 2 * halo), jnp.int32),
            pltpu.VMEM(neighbours.shape, jnp.int32),
            pltpu.VMEM(live_edges.shape, jnp.int32),
            pltpu.VMEM(w_rad.shape, F32),
            pltpu.VMEM(w_first.shape, BF16),
            pltpu.VMEM(w_second.shape, BF16),
            pltpu.VMEM(w_update.shape, BF16),
            pltpu.VMEM((1, channels), F32),
            pltpu.VMEM((2, 8, halo), F32),
            pltpu.VMEM((2, 8, halo), F32),
            pltpu.VMEM(halo_rows, BF16),
            pltpu.VMEM(halo_rows, BF16),
            pltpu.VMEM((walkers, atoms, channels), BF16),
            pltpu.VMEM((walkers, *halo_rows), BF16),
            pltpu.VMEM((walkers, *halo_rows), BF16),
            pltpu.VMEM((walkers, groups, edges, channels), F32),
            pltpu.VMEM((walkers, groups, edges, 2 * halo), BF16),
            pltpu.VMEM((2 * halo, atoms), BF16),
            pltpu.VMEM((2 * halo, LANES), BF16),
            pltpu.VMEM((walkers, groups, edges, LANES), BF16),
            pltpu.VMEM((edges, channels), F32),
            pltpu.VMEM((walkers, 3, slots, atoms), F32),
            pltpu.VMEM((4 * orders * slots, slots * channels), BF16),
            pltpu.VMEM((slots * 2 * channels, LANES), BF16),
            pltpu.VMEM((channels, 2 * channels), BF16),
            pltpu.VMEM((12 * groups, LANES), F32),
            pltpu.VMEM((walkers, 3, groups, LANES), F32),
            pltpu.VMEM((walkers, 2, 16, LANES), F32),
            pltpu.VMEM((walkers, 2, 16, LANES), F32),
            pltpu.VMEM((n_walk * walkers, 8, atoms), F32),
            pltpu.VMEM((LANES, slots * 2 * channels), BF16),
            pltpu.SemaphoreType.DMA((12,)),
            pltpu.SemaphoreType.DMA((copies,)),
            pltpu.SemaphoreType.DMA((copies,)),
        ],
        compiler_params=pltpu.CompilerParams(
            collective_id=0, has_side_effects=True, vmem_limit_bytes=58 * 2**20
        ),
    )(
        jnp.transpose(positions, (1, 0, 2)),
        jnp.transpose(velocities, (1, 0, 2)),
        species,
        masses[None],
        send_rows[None],
        neighbours,
        live_edges,
        w_rad,
        w_first,
        w_second,
        w_update,
        w_out[None],
        weights[None],
        bins[None],
        copy_src[None],
        copy_src,
    )
    return (
        jnp.transpose(out_positions, (1, 0, 2)),
        jnp.transpose(out_velocities, (1, 0, 2)),
        new_weights[0],
    )


def solution(mesh):
    in_specs = (
        P("walker", None, "domain"),
        P("walker", None, "domain"),
        P("domain", None),
        P("domain"),
        P("domain"),
        P("walker", None, "domain"),
        P("walker", None, "domain"),
        P(),
        P(),
        P(),
        P(),
        P(),
        P(),
        P(),
        P(),
    )
    out_specs = (P("walker", None, "domain"), P("walker", None, "domain"), P())
    return jax.shard_map(
        on_device, mesh=mesh, in_specs=in_specs, out_specs=out_specs, check_vma=False
    )
```

```python
import functools
import math

import jax
import jax.numpy as jnp
from jax import lax
from jax.experimental import pallas as pl
from jax.experimental.pallas import tpu as pltpu
from jax.sharding import PartitionSpec as P

OFFSET = 2.0
CUTOFF = 5.0
STEP = 0.2
LANES = 128
UNROLL = 4
MESH = pl.DeviceIdType.MESH
F32 = jnp.float32
BF16 = jnp.bfloat16


def lane_iota(shape):
    return lax.broadcasted_iota(jnp.int32, shape, len(shape) - 1)


def row_iota(shape):
    return lax.broadcasted_iota(jnp.int32, shape, 0)


def one_hot(column, width):
    rows = column.shape[0]
    wide = jnp.broadcast_to(column, (rows, LANES)).astype(jnp.int16)
    lanes = lane_iota((rows, LANES))
    one, zero = jnp.ones((rows, LANES), BF16), jnp.zeros((rows, LANES), BF16)
    return jnp.concatenate(
        [
            jnp.where(wide == (lanes + j * LANES).astype(jnp.int16), one, zero)
            for j in range(width // LANES)
        ],
        axis=1,
    )


def silu(x):
    half = 0.5 * x
    return half + half * jnp.tanh(half)


def split(x):
    head = x.astype(BF16).astype(F32)
    return head, x - head


def dot(a, b):
    return jnp.dot(a, b, preferred_element_type=F32)


def lane_lookup(rows, hi, lo):
    found = jnp.zeros(lo.shape, F32)
    for r, row in enumerate(rows):
        picked = jnp.take_along_axis(
            jnp.broadcast_to(row, lo.shape), lo, axis=1, mode="promise_in_bounds"
        )
        found = jnp.where(hi == r, picked, found)
    return found


def kernel(
    pos_h, vel_h, spc_h, mas_h, send_h, nbr_h, liv_h, wrad_h, w1_h, w2_h, wup_h, wout_h,
    wts, bns, csr, csr_s,
    opos, ovel, onw,
    pos, vel, spc, mas, send, nbr, liv, wrad, w1, w2, wup, wout,
    send_pos, halo_pos, send_spc, halo_spc, feat, send_feat, halo_feat, filt2, oh, send_oh,
    send_lo, low, gath, disp, wbig, wcat, acc, force, send_frc, recv_frc, every,
    load_sem, send_sem, recv_sem,
):
    n_walk, n_dom = lax.axis_size("walker"), lax.axis_size("domain")
    me_w, me_d = lax.axis_index("walker"), lax.axis_index("domain")
    left = lax.rem(me_d + n_dom - 1, n_dom)
    right = lax.rem(me_d + 1, n_dom)
    walkers, atoms = pos.shape[1], pos.shape[2]
    halo = send.shape[1] // 2
    groups = atoms // LANES
    slots = nbr.shape[1]
    tile_edges = slots * LANES
    peers = [(me_w, left), (me_w, right)]
    peers += [(lax.rem(me_w + o, n_walk), me_d) for o in range(1, n_walk)]

    barrier = pltpu.get_barrier_semaphore()
    for peer in peers:
        pl.semaphore_signal(barrier, inc=1, device_id=peer, device_id_type=MESH)

    loads = {}
    for i, (name, src, dst) in enumerate(
        [
            ("send", send_h, send),
            ("pos", pos_h, pos),
            ("spc", spc_h, spc),
            ("nbr", nbr_h, nbr),
            ("liv", liv_h, liv),
            ("wrad", wrad_h, wrad),
            ("w1", w1_h, w1),
            ("w2", w2_h, w2),
            ("wup", wup_h, wup),
            ("wout", wout_h, wout),
            ("vel", vel_h, vel),
            ("mas", mas_h, mas),
        ]
    ):
        loads[name] = pltpu.make_async_copy(src, dst, load_sem.at[i])
        loads[name].start()

    def remote(src, dst, sem, peer):
        return pltpu.make_async_remote_copy(
            src_ref=src,
            dst_ref=dst,
            send_sem=send_sem.at[sem],
            recv_sem=recv_sem.at[sem],
            device_id=peer,
            device_id_type=MESH,
        )

    def both_ways(src, dst, sem):
        copies = [
            remote(src.at[0], dst.at[1], sem, peers[0]),
            remote(src.at[1], dst.at[0], sem + 1, peers[1]),
        ]
        for copy in copies:
            copy.start()
        return copies

    loads["send"].wait()
    loads["pos"].wait()
    rows_out = jnp.concatenate(
        [send[:, g * LANES : (g + 1) * LANES] for g in range(groups)], axis=0
    )
    out_hi, out_lo = rows_out >> 7, rows_out & (LANES - 1)
    per_side = groups // 2
    for w in range(walkers):
        for c in range(3):
            table = [pos[c, w : w + 1, r * LANES : (r + 1) * LANES] for r in range(groups)]
            sent = lane_lookup(table, out_hi, out_lo)
            row = w * 3 + c
            for g in range(groups):
                q = g % per_side
                send_pos[g // per_side, row : row + 1, q * LANES : (q + 1) * LANES] = sent[g : g + 1]
    columns_out = jnp.transpose(rows_out)
    lo_out = jnp.transpose(out_lo)
    for g in range(groups):
        block = slice(g * LANES, (g + 1) * LANES)
        send_oh[block, :] = one_hot(columns_out[:, g : g + 1], atoms)
        send_lo[block, :] = one_hot(lo_out[:, g : g + 1], LANES)
    loads["spc"].wait()
    pl.semaphore_wait(barrier, len(peers))
    moves = both_ways(send_pos, halo_pos, 0)
    sent = dot(send_oh[...], spc[...]).astype(BF16)
    send_spc[0] = sent[:halo]
    send_spc[1] = sent[halo:]
    moves += both_ways(send_spc, halo_spc, 2)

    for name in ("nbr", "liv", "wrad", "w1", "w2", "wup", "wout", "vel", "mas"):
        loads[name].wait()

    def weights_by_slot():
        heads, tails = split(wrad[...])
        sub = row_iota((slots, LANES))
        for s in range(slots):
            blocks = []
            for piece in (heads, tails):
                for _ in range(2):
                    for k in range(piece.shape[0]):
                        line = jnp.broadcast_to(piece[k : k + 1, :], (slots, LANES))
                        blocks.append(jnp.where(sub == s, line, 0.0))
            wbig[:, s * LANES : (s + 1) * LANES] = jnp.concatenate(blocks, axis=0).astype(BF16)

    weights_by_slot()
    wcat[...] = jnp.zeros_like(wcat)
    for i in range(2):
        rows = slice(i * LANES, (i + 1) * LANES)
        wcat[rows, 2 * i * LANES : (2 * i + 1) * LANES] = w1[...]
        wcat[rows, (2 * i + 1) * LANES : (2 * i + 2) * LANES] = w2[...]

    count = wts.shape[1]
    square = (count, count)
    eye = (lane_iota(square) == row_iota(square)).astype(F32)

    def to_column(row):
        return jnp.sum(eye * row, axis=1, keepdims=True)

    def to_row(column):
        return jnp.sum(eye * column, axis=0, keepdims=True)

    w_row, b_row = wts[...], bns[...].astype(F32)
    chosen = (to_column(csr[...].astype(F32)) == lane_iota(square).astype(F32)).astype(F32)
    src_w = jnp.sum(chosen * w_row, axis=1, keepdims=True)
    src_b = jnp.sum(chosen * b_row, axis=1, keepdims=True)
    mass = jnp.sum((src_b == b_row).astype(F32) * w_row, axis=1, keepdims=True)
    share = jnp.sum((src_b == to_row(src_b)).astype(F32) * to_row(src_w), axis=1, keepdims=True)
    onw[...] = to_row(mass * src_w / share)

    def build(w, t):
        at = pl.ds(pl.multiple_of(t * LANES, LANES), LANES)
        ids = nbr[w, :, at]
        key_t = jnp.transpose(jnp.where(liv[w, :, at] != 0, ids & (halo - 1), -1))
        lo_t = jnp.transpose(ids & (LANES - 1))
        for s in range(slots):
            block = slice(s * LANES, (s + 1) * LANES)
            oh[w, t, block, :] = one_hot(key_t[:, s : s + 1], halo)
            low[w, t, block, :] = one_hot(lo_t[:, s : s + 1], LANES)

    def gather_rows(w, t, lane, ids, own, near):
        odd_t = jnp.transpose((ids >> 9) & 1)
        far_t = jnp.transpose(ids >> 10)
        table = jnp.concatenate([own[:halo], own[halo:], near[0], near[1]], axis=1)
        both = dot(oh[w, t], table)
        for s in range(slots):
            block = slice(s * LANES, (s + 1) * LANES)
            odd = jnp.broadcast_to(odd_t[:, s : s + 1], (LANES, LANES)) != 0
            far = jnp.broadcast_to(far_t[:, s : s + 1], (LANES, LANES)) != 0
            parts = [both[block, i * LANES : (i + 1) * LANES] for i in range(4)]
            gath[lane, block, :] = jnp.where(
                far, jnp.where(odd, parts[3], parts[2]), jnp.where(odd, parts[1], parts[0])
            )

    def geometry(w, at, ids):
        hi, lo = ids >> 7, ids & (LANES - 1)
        square_sum = None
        for c in range(3):
            table = [pos[c, w : w + 1, r * LANES : (r + 1) * LANES] for r in range(groups)]
            for side in range(2):
                shift = 0.0 if c else (OFFSET if side else -OFFSET)
                for q in range(per_side):
                    row = w * 3 + c
                    table.append(
                        halo_pos[side, row : row + 1, q * LANES : (q + 1) * LANES] + shift
                    )
            delta = lane_lookup(table, hi, lo) - pos[c, w : w + 1, at]
            disp[w, c, :, at] = delta
            square_sum = delta * delta if c == 0 else square_sum + delta * delta
        scaled = jnp.sqrt(square_sum) / CUTOFF
        envelope = jnp.square(jnp.maximum(0.0, 1.0 - scaled * scaled))
        first = jnp.cos(jnp.minimum(scaled, 1.0) * math.pi)
        waves = [first, 2.0 * first * first - 1.0]
        while len(waves) < wrad.shape[0]:
            waves.append(2.0 * first * waves[-1] - waves[-2])
        pieces = [split(wave * envelope) for wave in waves]
        stacked = jnp.concatenate([p[0] for p in pieces] + [p[1] for p in pieces], axis=0)
        turned = jnp.transpose(stacked).astype(BF16)
        return jnp.concatenate([turned, turned], axis=1)

    def first_gather(w, t, lane):
        at = pl.ds(pl.multiple_of(t * LANES, LANES), LANES)
        ids = nbr[w, :, at]
        gather_rows(w, t, lane, ids, spc[...], halo_spc)
        return geometry(w, at, ids)

    def first_head(w, t, lane, basis):
        at = pl.ds(pl.multiple_of(t * LANES, LANES), LANES)
        total = jnp.zeros((LANES, LANES), F32)
        for s in range(0, slots, 4):
            radial = silu(dot(basis, wbig[:, s * LANES : (s + 4) * LANES])).astype(BF16)
            for i in range(4):
                if i % 2 == 0:
                    pair = dot(radial[:, i * LANES : (i + 2) * LANES], wcat[...])
                block = slice((s + i) * LANES, (s + i + 1) * LANES)
                column = (i % 2) * 2 * LANES
                filt2[w, t, block, :] = pair[:, column + LANES : column + 2 * LANES]
                total = total + pair[:, column : column + LANES] * gath[lane, block, :]
        updated = dot(total.astype(BF16), wup[...])
        feat[w, at, :] = (spc[at, :].astype(F32) + silu(updated)).astype(BF16)

    def second_gather(w, t, lane):
        at = pl.ds(pl.multiple_of(t * LANES, LANES), LANES)
        ids = nbr[w, :, at]
        gather_rows(w, t, lane, ids, feat[w], halo_feat[w])
        return ids

    def second_head(w, t, lane, ids):
        at = pl.ds(pl.multiple_of(t * LANES, LANES), LANES)
        own = feat[w, at, :].astype(F32) * wout[...]
        lanes = lane_iota((LANES, LANES))
        by_slot = jnp.zeros((LANES, LANES), F32)
        for s in range(slots):
            block = slice(s * LANES, (s + 1) * LANES)
            product = filt2[w, t, block, :] * own * gath[lane, block, :]
            by_slot = jnp.where(lanes == s, jnp.sum(product, axis=1, keepdims=True), by_slot)
        coupling = jnp.transpose(by_slot)[:slots]
        hi = ids >> 7
        pieces = []
        for c in range(3):
            pair = coupling * disp[w, c, :, at]
            force[w, c, pl.ds(t, 1), :] = jnp.sum(pair, axis=0, keepdims=True)
            pieces.append(split(pair))
        acc[...] += dot(spread_left(pieces, hi, 2 * groups), low[w, t])

    def spread_left(pieces, hi, high_count):
        sub = row_iota((high_count, LANES))
        out = []
        for s in range(hi.shape[0]):
            here = jnp.broadcast_to(hi[s : s + 1], (high_count, LANES)) == sub
            rows = [
                jnp.where(here, jnp.broadcast_to(x[p][s : s + 1], (high_count, LANES)), 0.0)
                for p in range(2)
                for x in pieces
            ]
            out.append(jnp.concatenate(rows, axis=0).astype(BF16))
        return jnp.concatenate(out, axis=1)

    def loop(gather, head, w):
        def step(i, carry):
            held = gather(w, i * UNROLL, 0)
            for j in range(UNROLL):
                later = gather(w, i * UNROLL + j + 1, j + 1) if j + 1 < UNROLL else None
                head(w, i * UNROLL + j, j, held)
                held = later
            return carry

        lax.fori_loop(0, groups // UNROLL, step, 0)

    def build_all(w):
        def step(i, carry):
            for j in range(2):
                build(w, 2 * i + j)
            return carry

        lax.fori_loop(0, groups // 2, step, 0)

    for w in range(walkers):
        build_all(w)
    for copy in moves:
        copy.wait()
    feat_moves = []
    for w in range(walkers):
        loop(first_gather, first_head, w)
        sent = dot(send_oh[...], feat[w]).astype(BF16)
        send_feat[w, 0] = sent[:halo]
        send_feat[w, 1] = sent[halo:]
        feat_moves.append(both_ways(send_feat.at[w], halo_feat.at[w], 4 + 2 * w))

    force_moves = []
    high = 2 * groups
    for w in range(walkers):
        for copy in feat_moves[w]:
            copy.wait()
        acc[...] = jnp.zeros_like(acc)
        loop(second_gather, second_head, w)
        reaction = acc[: 3 * high] + acc[3 * high :]
        for c in range(3):
            force[w, c] = force[w, c] - reaction[c * high : c * high + groups]
            for side in range(2):
                start = c * high + groups + side * per_side
                send_frc[w, side, c * per_side : (c + 1) * per_side, :] = -reaction[
                    start : start + per_side
                ]
        base = 4 + 2 * walkers + 2 * w
        force_moves.append(both_ways(send_frc.at[w], recv_frc.at[w], base))

    state_moves = []
    for w in range(walkers):
        for copy in force_moves[w]:
            copy.wait()
        pieces = []
        for c in range(3):
            rows = slice(c * per_side, (c + 1) * per_side)
            pieces.append(
                split(jnp.concatenate([recv_frc[w, 0, rows, :], recv_frc[w, 1, rows, :]], axis=0))
            )
        back = dot(spread_left(pieces, out_hi, groups), send_lo[...])
        for c in range(3):
            total = force[w, c] + (
                back[c * groups : (c + 1) * groups]
                + back[(3 + c) * groups : (4 + c) * groups]
            )
            flat = jnp.concatenate([total[g : g + 1] for g in range(groups)], axis=1)
            stepped = vel[c, w : w + 1, :] + STEP * flat / mas[...]
            every[w, c : c + 1, :] = pos[c, w : w + 1, :] + STEP * stepped
            every[w, 3 + c : 4 + c, :] = stepped
        for o in range(1, n_walk):
            base = 4 + 4 * walkers + w * (n_walk - 1) + o - 1
            copy = remote(every.at[w], every.at[o * walkers + w], base, peers[1 + o])
            copy.start()
            state_moves.append(copy)
    for copy in state_moves:
        copy.wait()
    for k in range(walkers):
        source = csr_s[me_w * walkers + k]
        behind = lax.rem(me_w - lax.div(source, walkers) + n_walk, n_walk)
        picked = every[behind * walkers + lax.rem(source, walkers)]
        for c in range(3):
            opos[c, k : k + 1, :] = picked[c : c + 1]
            ovel[c, k : k + 1, :] = picked[3 + c : 4 + c]


def on_device(
    positions,
    velocities,
    species,
    masses,
    send_rows,
    neighbours,
    live_edges,
    w_rad,
    w_first,
    w_second,
    w_update,
    w_out,
    weights,
    bins,
    copy_src,
):
    walkers, _, atoms = positions.shape
    channels = species.shape[1]
    halo = send_rows.shape[0] // 2
    groups = atoms // LANES
    slots = neighbours.shape[1]
    orders = w_rad.shape[0]
    n_walk = lax.axis_size("walker")
    edges = slots * LANES
    copies = 4 + 4 * walkers + walkers * (n_walk - 1)
    by_component = (3, walkers, atoms)
    hbm = pl.BlockSpec(memory_space=pltpu.HBM)
    vmem = pl.BlockSpec(memory_space=pltpu.VMEM)
    smem = pl.BlockSpec(memory_space=pltpu.SMEM)
    halo_rows = (2, halo, channels)
    out_positions, out_velocities, new_weights = pl.pallas_call(
        kernel,
        out_shape=(
            jax.ShapeDtypeStruct(by_component, F32),
            jax.ShapeDtypeStruct(by_component, F32),
            jax.ShapeDtypeStruct((1, weights.shape[0]), F32),
        ),
        in_specs=[hbm] * 12 + [vmem] * 3 + [smem],
        out_specs=(vmem, vmem, vmem),
        scratch_shapes=[
            pltpu.VMEM(by_component, F32),
            pltpu.VMEM(by_component, F32),
            pltpu.VMEM(species.shape, BF16),
            pltpu.VMEM((1, atoms), F32),
            pltpu.VMEM((1, 2 * halo), jnp.int32),
            pltpu.VMEM(neighbours.shape, jnp.int32),
            pltpu.VMEM(live_edges.shape, jnp.int32),
            pltpu.VMEM(w_rad.shape, F32),
            pltpu.VMEM(w_first.shape, BF16),
            pltpu.VMEM(w_second.shape, BF16),
            pltpu.VMEM(w_update.shape, BF16),
            pltpu.VMEM((1, channels), F32),
            pltpu.VMEM((2, 8, halo), F32),
            pltpu.VMEM((2, 8, halo), F32),
            pltpu.VMEM(halo_rows, BF16),
            pltpu.VMEM(halo_rows, BF16),
            pltpu.VMEM((walkers, atoms, channels), BF16),
            pltpu.VMEM((walkers, *halo_rows), BF16),
            pltpu.VMEM((walkers, *halo_rows), BF16),
            pltpu.VMEM((walkers, groups, edges, channels), F32),
            pltpu.VMEM((walkers, groups, edges, halo), BF16),
            pltpu.VMEM((2 * halo, atoms), BF16),
            pltpu.VMEM((2 * halo, LANES), BF16),
            pltpu.VMEM((walkers, groups, edges, LANES), BF16),
            pltpu.VMEM((UNROLL, edges, channels), F32),
            pltpu.VMEM((walkers, 3, slots, atoms), F32),
            pltpu.VMEM((4 * orders * slots, slots * channels), BF16),
            pltpu.VMEM((2 * channels, 4 * channels), BF16),
            pltpu.VMEM((12 * groups, LANES), F32),
            pltpu.VMEM((walkers, 3, groups, LANES), F32),
            pltpu.VMEM((walkers, 2, 16, LANES), F32),
            pltpu.VMEM((walkers, 2, 16, LANES), F32),
            pltpu.VMEM((n_walk * walkers, 8, atoms), F32),
            pltpu.SemaphoreType.DMA((12,)),
            pltpu.SemaphoreType.DMA((copies,)),
            pltpu.SemaphoreType.DMA((copies,)),
        ],
        compiler_params=pltpu.CompilerParams(
            collective_id=0, has_side_effects=True, vmem_limit_bytes=58 * 2**20
        ),
    )(
        jnp.transpose(positions, (1, 0, 2)),
        jnp.transpose(velocities, (1, 0, 2)),
        species,
        masses[None],
        send_rows[None],
        neighbours,
        live_edges,
        w_rad,
        w_first,
        w_second,
        w_update,
        w_out[None],
        weights[None],
        bins[None],
        copy_src[None],
        copy_src,
    )
    return (
        jnp.transpose(out_positions, (1, 0, 2)),
        jnp.transpose(out_velocities, (1, 0, 2)),
        new_weights[0],
    )


def solution(mesh):
    in_specs = (
        P("walker", None, "domain"),
        P("walker", None, "domain"),
        P("domain", None),
        P("domain"),
        P("domain"),
        P("walker", None, "domain"),
        P("walker", None, "domain"),
        P(),
        P(),
        P(),
        P(),
        P(),
        P(),
        P(),
        P(),
    )
    out_specs = (P("walker", None, "domain"), P("walker", None, "domain"), P())
    return jax.shard_map(
        on_device, mesh=mesh, in_specs=in_specs, out_specs=out_specs, check_vma=False
    )
```

```python
import functools
import math

import jax
import jax.numpy as jnp
from jax import lax
from jax.experimental import pallas as pl
from jax.experimental.pallas import tpu as pltpu
from jax.sharding import PartitionSpec as P

OFFSET = 2.0
CUTOFF = 5.0
STEP = 0.2
LANES = 128
UNROLL = 4
MESH = pl.DeviceIdType.MESH
F32 = jnp.float32
BF16 = jnp.bfloat16


def lane_iota(shape):
    return lax.broadcasted_iota(jnp.int32, shape, len(shape) - 1)


def row_iota(shape):
    return lax.broadcasted_iota(jnp.int32, shape, 0)


def one_hot(column, width):
    rows = column.shape[0]
    wide = jnp.broadcast_to(column, (rows, LANES)).astype(jnp.int16)
    lanes = lane_iota((rows, LANES))
    one, zero = jnp.ones((rows, LANES), BF16), jnp.zeros((rows, LANES), BF16)
    return jnp.concatenate(
        [
            jnp.where(wide == (lanes + j * LANES).astype(jnp.int16), one, zero)
            for j in range(width // LANES)
        ],
        axis=1,
    )


def silu(x):
    half = 0.5 * x
    return half + half * jnp.tanh(half)


def split(x):
    head = x.astype(BF16).astype(F32)
    return head, x - head


def dot(a, b):
    return jnp.dot(a, b, preferred_element_type=F32)


def choose(both, column):
    number = jnp.broadcast_to(column, (both.shape[0], LANES))
    odd, far = (number & 1) != 0, number >= 2
    parts = [both[:, i * LANES : (i + 1) * LANES] for i in range(4)]
    return jnp.where(far, jnp.where(odd, parts[3], parts[2]), jnp.where(odd, parts[1], parts[0]))


def lane_lookup(rows, hi, lo):
    found = jnp.zeros(lo.shape, F32)
    for r, row in enumerate(rows):
        picked = jnp.take_along_axis(
            jnp.broadcast_to(row, lo.shape), lo, axis=1, mode="promise_in_bounds"
        )
        found = jnp.where(hi == r, picked, found)
    return found


def kernel(
    pos_h, vel_h, spc_h, mas_h, send_h, nbr_h, liv_h, wrad_h, w1_h, w2_h, wup_h, wout_h,
    wts, bns, csr, csr_s,
    opos, ovel, onw,
    pos, vel, spc, mas, send, nbr, liv, wrad, w1, w2, wup, wout,
    send_pos, halo_pos, send_spc, halo_spc, feat, send_feat, halo_feat, filt2, oh, send_oh,
    send_lo, low, gath, disp, wbig, wcat, acc, force, send_frc, recv_frc, every,
    load_sem, send_sem, recv_sem,
):
    n_walk, n_dom = lax.axis_size("walker"), lax.axis_size("domain")
    me_w, me_d = lax.axis_index("walker"), lax.axis_index("domain")
    left = lax.rem(me_d + n_dom - 1, n_dom)
    right = lax.rem(me_d + 1, n_dom)
    walkers, atoms = pos.shape[1], pos.shape[2]
    halo = send.shape[1] // 2
    groups = atoms // LANES
    slots = nbr.shape[1]
    tile_edges = slots * LANES
    peers = [(me_w, left), (me_w, right)]
    ranks = [me_w] + [lax.rem(me_w + o, n_walk) for o in range(1, n_walk)]
    peers += [(rank, me_d) for rank in ranks[1:]]
    peers += [(rank, side) for rank in ranks[1:] for side in (left, right)]

    barrier = pltpu.get_barrier_semaphore()
    for peer in peers:
        pl.semaphore_signal(barrier, inc=1, device_id=peer, device_id_type=MESH)

    loads = {}
    for i, (name, src, dst) in enumerate(
        [
            ("send", send_h, send),
            ("pos", pos_h, pos),
            ("spc", spc_h, spc),
            ("nbr", nbr_h, nbr),
            ("liv", liv_h, liv),
            ("wrad", wrad_h, wrad),
            ("w1", w1_h, w1),
            ("w2", w2_h, w2),
            ("wup", wup_h, wup),
            ("wout", wout_h, wout),
            ("vel", vel_h, vel),
            ("mas", mas_h, mas),
        ]
    ):
        loads[name] = pltpu.make_async_copy(src, dst, load_sem.at[i])
        loads[name].start()

    def remote(src, dst, sem, peer):
        return pltpu.make_async_remote_copy(
            src_ref=src,
            dst_ref=dst,
            send_sem=send_sem.at[sem],
            recv_sem=recv_sem.at[sem],
            device_id=peer,
            device_id_type=MESH,
        )

    def both_ways(src, dst, sem):
        copies = [
            remote(src.at[0], dst.at[1], sem, peers[0]),
            remote(src.at[1], dst.at[0], sem + 1, peers[1]),
        ]
        for copy in copies:
            copy.start()
        return copies

    loads["send"].wait()
    loads["pos"].wait()
    rows_out = jnp.concatenate(
        [send[:, g * LANES : (g + 1) * LANES] for g in range(groups)], axis=0
    )
    out_hi, out_lo = rows_out >> 7, rows_out & (LANES - 1)
    per_side = groups // 2
    for w in range(walkers):
        for c in range(3):
            table = [pos[c, w : w + 1, r * LANES : (r + 1) * LANES] for r in range(groups)]
            sent = lane_lookup(table, out_hi, out_lo)
            row = w * 3 + c
            for g in range(groups):
                q = g % per_side
                send_pos[g // per_side, row : row + 1, q * LANES : (q + 1) * LANES] = sent[g : g + 1]
    quarter = atoms // 4
    columns_out = jnp.transpose(rows_out & (quarter - 1))
    quarters_out = jnp.transpose(rows_out >> 8)
    for g in range(groups):
        block = slice(g * LANES, (g + 1) * LANES)
        hot = one_hot(columns_out[:, g : g + 1], quarter)
        send_oh[block, :] = hot
        send_lo[block, :] = hot[:, :LANES] + hot[:, LANES:]

    def send_gather(rows, target):
        table = jnp.concatenate(
            [rows[i * quarter : (i + 1) * quarter] for i in range(4)], axis=1
        )
        both = dot(send_oh[...], table)
        for g in range(groups):
            picked = choose(both[g * LANES : (g + 1) * LANES], quarters_out[:, g : g + 1])
            q = g % per_side
            target[g // per_side, q * LANES : (q + 1) * LANES, :] = picked.astype(BF16)

    loads["spc"].wait()
    loads["vel"].wait()
    for w in range(walkers):
        for c in range(3):
            every[w, c : c + 1, :] = pos[c, w : w + 1, :]
            every[w, 3 + c : 4 + c, :] = vel[c, w : w + 1, :]
    pl.semaphore_wait(barrier, len(peers))
    moves = both_ways(send_pos, halo_pos, 0)
    send_gather(spc[...], send_spc)
    moves += both_ways(send_spc, halo_spc, 2)
    late_moves = []
    sems = iter(range(4 + 2 * walkers, send_sem.shape[0]))

    def send_late(src, dst, peer):
        copy = remote(src, dst, next(sems), peer)
        copy.start()
        late_moves.append(copy)

    for o in range(1, n_walk):
        mine, theirs = pl.ds(0, walkers), pl.ds(o * walkers, walkers)
        send_late(every.at[mine], every.at[theirs], (ranks[o], me_d))

    for name in ("nbr", "liv", "wrad", "w1", "w2", "wup", "wout", "mas"):
        loads[name].wait()

    def weights_by_slot():
        heads, tails = split(wrad[...])
        sub = row_iota((slots, LANES))
        for s in range(slots):
            blocks = []
            for piece in (heads, tails):
                for _ in range(2):
                    for k in range(piece.shape[0]):
                        line = jnp.broadcast_to(piece[k : k + 1, :], (slots, LANES))
                        blocks.append(jnp.where(sub == s, line, 0.0))
            wbig[:, s * LANES : (s + 1) * LANES] = jnp.concatenate(blocks, axis=0).astype(BF16)

    weights_by_slot()
    wcat[...] = jnp.zeros_like(wcat)
    for i in range(2):
        rows = slice(i * LANES, (i + 1) * LANES)
        wcat[rows, 2 * i * LANES : (2 * i + 1) * LANES] = w1[...]
        wcat[rows, (2 * i + 1) * LANES : (2 * i + 2) * LANES] = w2[...]

    count = wts.shape[1]
    square = (count, count)
    eye = (lane_iota(square) == row_iota(square)).astype(F32)

    def to_column(row):
        return jnp.sum(eye * row, axis=1, keepdims=True)

    def to_row(column):
        return jnp.sum(eye * column, axis=0, keepdims=True)

    w_row, b_row = wts[...], bns[...].astype(F32)
    chosen = (to_column(csr[...].astype(F32)) == lane_iota(square).astype(F32)).astype(F32)
    src_w = jnp.sum(chosen * w_row, axis=1, keepdims=True)
    src_b = jnp.sum(chosen * b_row, axis=1, keepdims=True)
    mass = jnp.sum((src_b == b_row).astype(F32) * w_row, axis=1, keepdims=True)
    share = jnp.sum((src_b == to_row(src_b)).astype(F32) * to_row(src_w), axis=1, keepdims=True)
    onw[...] = to_row(mass * src_w / share)

    def build(w, t):
        at = pl.ds(pl.multiple_of(t * LANES, LANES), LANES)
        ids = nbr[w, :, at]
        key_t = jnp.transpose(jnp.where(liv[w, :, at] != 0, ids & (halo - 1), -1))
        for s in range(slots):
            block = slice(s * LANES, (s + 1) * LANES)
            hot = one_hot(key_t[:, s : s + 1], halo)
            oh[w, t, block, :] = hot
            parts = [hot[:, i * LANES : (i + 1) * LANES] for i in range(halo // LANES)]
            low[w, t, block, :] = functools.reduce(jnp.add, parts)

    def gather_rows(w, t, lane, ids, own, near):
        quarter_t = jnp.transpose(ids >> 9)
        table = jnp.concatenate([own[:halo], own[halo:], near[0], near[1]], axis=1)
        both = dot(oh[w, t], table)
        for s in range(slots):
            block = slice(s * LANES, (s + 1) * LANES)
            gath[lane, block, :] = choose(both[block], quarter_t[:, s : s + 1])

    def geometry(w, at, ids):
        hi, lo = ids >> 7, ids & (LANES - 1)
        square_sum = None
        for c in range(3):
            table = [pos[c, w : w + 1, r * LANES : (r + 1) * LANES] for r in range(groups)]
            for side in range(2):
                shift = 0.0 if c else (OFFSET if side else -OFFSET)
                for q in range(per_side):
                    row = w * 3 + c
                    table.append(
                        halo_pos[side, row : row + 1, q * LANES : (q + 1) * LANES] + shift
                    )
            delta = lane_lookup(table, hi, lo) - pos[c, w : w + 1, at]
            disp[w, c, :, at] = delta
            square_sum = delta * delta if c == 0 else square_sum + delta * delta
        scaled = jnp.sqrt(square_sum) / CUTOFF
        envelope = jnp.square(jnp.maximum(0.0, 1.0 - scaled * scaled))
        first = jnp.cos(jnp.minimum(scaled, 1.0) * math.pi)
        waves = [first, 2.0 * first * first - 1.0]
        while len(waves) < wrad.shape[0]:
            waves.append(2.0 * first * waves[-1] - waves[-2])
        pieces = [split(wave * envelope) for wave in waves]
        stacked = jnp.concatenate([p[0] for p in pieces] + [p[1] for p in pieces], axis=0)
        turned = jnp.transpose(stacked).astype(BF16)
        return jnp.concatenate([turned, turned], axis=1)

    def first_gather(w, t, lane):
        at = pl.ds(pl.multiple_of(t * LANES, LANES), LANES)
        ids = nbr[w, :, at]
        gather_rows(w, t, lane, ids, spc[...], halo_spc)
        return geometry(w, at, ids)

    def first_head(w, t, lane, basis):
        at = pl.ds(pl.multiple_of(t * LANES, LANES), LANES)
        total = jnp.zeros((LANES, LANES), F32)
        for s in range(0, slots, 4):
            radial = silu(dot(basis, wbig[:, s * LANES : (s + 4) * LANES])).astype(BF16)
            for i in range(4):
                if i % 2 == 0:
                    pair = dot(radial[:, i * LANES : (i + 2) * LANES], wcat[...])
                block = slice((s + i) * LANES, (s + i + 1) * LANES)
                column = (i % 2) * 2 * LANES
                filt2[w, t, block, :] = pair[:, column + LANES : column + 2 * LANES]
                total = total + pair[:, column : column + LANES] * gath[lane, block, :]
        updated = dot(total.astype(BF16), wup[...])
        feat[w, at, :] = (spc[at, :].astype(F32) + silu(updated)).astype(BF16)

    def second_gather(w, t, lane):
        at = pl.ds(pl.multiple_of(t * LANES, LANES), LANES)
        ids = nbr[w, :, at]
        gather_rows(w, t, lane, ids, feat[w], halo_feat[w])
        return ids

    def second_head(w, t, lane, ids):
        at = pl.ds(pl.multiple_of(t * LANES, LANES), LANES)
        own = feat[w, at, :].astype(F32) * wout[...]
        lanes = lane_iota((LANES, LANES))
        by_slot = jnp.zeros((LANES, LANES), F32)
        for s in range(slots):
            block = slice(s * LANES, (s + 1) * LANES)
            product = filt2[w, t, block, :] * own * gath[lane, block, :]
            by_slot = jnp.where(lanes == s, jnp.sum(product, axis=1, keepdims=True), by_slot)
        coupling = jnp.transpose(by_slot)[:slots]
        hi = ids >> 7
        pieces = []
        for c in range(3):
            pair = coupling * disp[w, c, :, at]
            force[w, pl.ds(c * groups + t, 1), :] = jnp.sum(pair, axis=0, keepdims=True)
            pieces.append(split(pair))
        acc[...] += dot(spread_left(pieces, hi, 2 * groups), low[w, t])

    def spread_left(pieces, hi, high_count):
        sub = row_iota((high_count, LANES))
        out = []
        for s in range(hi.shape[0]):
            here = jnp.broadcast_to(hi[s : s + 1], (high_count, LANES)) == sub
            rows = [
                jnp.where(here, jnp.broadcast_to(x[p][s : s + 1], (high_count, LANES)), 0.0)
                for p in range(2)
                for x in pieces
            ]
            out.append(jnp.concatenate(rows, axis=0).astype(BF16))
        return jnp.concatenate(out, axis=1)

    def loop(gather, head, w):
        def step(i, carry):
            held = gather(w, i * UNROLL, 0)
            for j in range(UNROLL):
                later = gather(w, i * UNROLL + j + 1, j + 1) if j + 1 < UNROLL else None
                head(w, i * UNROLL + j, j, held)
                held = later
            return carry

        lax.fori_loop(0, groups // UNROLL, step, 0)

    def build_all(w):
        def step(i, carry):
            for j in range(2):
                build(w, 2 * i + j)
            return carry

        lax.fori_loop(0, groups // 2, step, 0)

    for w in range(walkers):
        build_all(w)
    for copy in moves:
        copy.wait()
    feat_moves = []
    for w in range(walkers):
        loop(first_gather, first_head, w)
        send_gather(feat[w], send_feat.at[w])
        feat_moves.append(both_ways(send_feat.at[w], halo_feat.at[w], 4 + 2 * w))

    high = 2 * groups
    for w in range(walkers):
        for copy in feat_moves[w]:
            copy.wait()
        acc[...] = jnp.zeros_like(acc)
        loop(second_gather, second_head, w)
        reaction = acc[: 3 * high] + acc[3 * high :]
        for c in range(3):
            for side in range(2):
                start = c * high + groups + side * per_side
                send_frc[w, side, c * per_side : (c + 1) * per_side, :] = -reaction[
                    start : start + per_side
                ]
            force[w, c * groups : (c + 1) * groups, :] = (
                force[w, c * groups : (c + 1) * groups, :] - reaction[c * high : c * high + groups]
            )
        for o in range(n_walk):
            slot = o * walkers + w
            send_late(send_frc.at[w, 0], recv_frc.at[slot, 1], (ranks[o], left))
            send_late(send_frc.at[w, 1], recv_frc.at[slot, 0], (ranks[o], right))
            if o:
                send_late(force.at[w], force.at[slot], (ranks[o], me_d))
    for copy in late_moves:
        copy.wait()
    for k in range(walkers):
        source = csr_s[me_w * walkers + k]
        behind = lax.rem(me_w - lax.div(source, walkers) + n_walk, n_walk)
        slot = behind * walkers + lax.rem(source, walkers)
        state, own, back = every[slot], force[slot], recv_frc[slot]
        pieces = []
        for c in range(3):
            rows = slice(c * per_side, (c + 1) * per_side)
            pieces.append(split(jnp.concatenate([back[0, rows], back[1, rows]], axis=0)))
        spread_back = dot(spread_left(pieces, out_hi, groups), send_lo[...])
        for c in range(3):
            total = own[c * groups : (c + 1) * groups] + (
                spread_back[c * groups : (c + 1) * groups]
                + spread_back[(3 + c) * groups : (4 + c) * groups]
            )
            flat = jnp.concatenate([total[g : g + 1] for g in range(groups)], axis=1)
            stepped = state[3 + c : 4 + c] + STEP * flat / mas[...]
            opos[c, k : k + 1, :] = state[c : c + 1] + STEP * stepped
            ovel[c, k : k + 1, :] = stepped


def on_device(
    positions,
    velocities,
    species,
    masses,
    send_rows,
    neighbours,
    live_edges,
    w_rad,
    w_first,
    w_second,
    w_update,
    w_out,
    weights,
    bins,
    copy_src,
):
    walkers, _, atoms = positions.shape
    channels = species.shape[1]
    halo = send_rows.shape[0] // 2
    groups = atoms // LANES
    slots = neighbours.shape[1]
    orders = w_rad.shape[0]
    n_walk = lax.axis_size("walker")
    edges = slots * LANES
    copies = 4 + 2 * walkers + (n_walk - 1) + walkers * (3 * n_walk - 1)
    by_component = (3, walkers, atoms)
    hbm = pl.BlockSpec(memory_space=pltpu.HBM)
    vmem = pl.BlockSpec(memory_space=pltpu.VMEM)
    smem = pl.BlockSpec(memory_space=pltpu.SMEM)
    halo_rows = (2, halo, channels)
    out_positions, out_velocities, new_weights = pl.pallas_call(
        kernel,
        out_shape=(
            jax.ShapeDtypeStruct(by_component, F32),
            jax.ShapeDtypeStruct(by_component, F32),
            jax.ShapeDtypeStruct((1, weights.shape[0]), F32),
        ),
        in_specs=[hbm] * 12 + [vmem] * 3 + [smem],
        out_specs=(vmem, vmem, vmem),
        scratch_shapes=[
            pltpu.VMEM(by_component, F32),
            pltpu.VMEM(by_component, F32),
            pltpu.VMEM(species.shape, BF16),
            pltpu.VMEM((1, atoms), F32),
            pltpu.VMEM((1, 2 * halo), jnp.int32),
            pltpu.VMEM(neighbours.shape, jnp.int32),
            pltpu.VMEM(live_edges.shape, jnp.int32),
            pltpu.VMEM(w_rad.shape, F32),
            pltpu.VMEM(w_first.shape, BF16),
            pltpu.VMEM(w_second.shape, BF16),
            pltpu.VMEM(w_update.shape, BF16),
            pltpu.VMEM((1, channels), F32),
            pltpu.VMEM((2, 8, halo), F32),
            pltpu.VMEM((2, 8, halo), F32),
            pltpu.VMEM(halo_rows, BF16),
            pltpu.VMEM(halo_rows, BF16),
            pltpu.VMEM((walkers, atoms, channels), BF16),
            pltpu.VMEM((walkers, *halo_rows), BF16),
            pltpu.VMEM((walkers, *halo_rows), BF16),
            pltpu.VMEM((walkers, groups, edges, channels), F32),
            pltpu.VMEM((walkers, groups, edges, halo), BF16),
            pltpu.VMEM((2 * halo, atoms // 4), BF16),
            pltpu.VMEM((2 * halo, LANES), BF16),
            pltpu.VMEM((walkers, groups, edges, LANES), BF16),
            pltpu.VMEM((UNROLL, edges, channels), F32),
            pltpu.VMEM((walkers, 3, slots, atoms), F32),
            pltpu.VMEM((4 * orders * slots, slots * channels), BF16),
            pltpu.VMEM((2 * channels, 4 * channels), BF16),
            pltpu.VMEM((12 * groups, LANES), F32),
            pltpu.VMEM((n_walk * walkers, 3 * groups, LANES), F32),
            pltpu.VMEM((walkers, 2, 16, LANES), F32),
            pltpu.VMEM((n_walk * walkers, 2, 16, LANES), F32),
            pltpu.VMEM((n_walk * walkers, 8, atoms), F32),
            pltpu.SemaphoreType.DMA((12,)),
            pltpu.SemaphoreType.DMA((copies,)),
            pltpu.SemaphoreType.DMA((copies,)),
        ],
        compiler_params=pltpu.CompilerParams(
            collective_id=0, has_side_effects=True, vmem_limit_bytes=58 * 2**20
        ),
    )(
        jnp.transpose(positions, (1, 0, 2)),
        jnp.transpose(velocities, (1, 0, 2)),
        species,
        masses[None],
        send_rows[None],
        neighbours,
        live_edges,
        w_rad,
        w_first,
        w_second,
        w_update,
        w_out[None],
        weights[None],
        bins[None],
        copy_src[None],
        copy_src,
    )
    return (
        jnp.transpose(out_positions, (1, 0, 2)),
        jnp.transpose(out_velocities, (1, 0, 2)),
        new_weights[0],
    )


def solution(mesh):
    in_specs = (
        P("walker", None, "domain"),
        P("walker", None, "domain"),
        P("domain", None),
        P("domain"),
        P("domain"),
        P("walker", None, "domain"),
        P("walker", None, "domain"),
        P(),
        P(),
        P(),
        P(),
        P(),
        P(),
        P(),
        P(),
    )
    out_specs = (P("walker", None, "domain"), P("walker", None, "domain"), P())
    return jax.shard_map(
        on_device, mesh=mesh, in_specs=in_specs, out_specs=out_specs, check_vma=False
    )
```

```python
import functools
import math

import jax
import jax.numpy as jnp
from jax import lax
from jax.experimental import pallas as pl
from jax.experimental.pallas import tpu as pltpu
from jax.sharding import PartitionSpec as P

OFFSET = 2.0
CUTOFF = 5.0
STEP = 0.2
LANES = 128
UNROLL = 4
AHEAD = 2
CHUNK = 4
MESH = pl.DeviceIdType.MESH
F32 = jnp.float32
BF16 = jnp.bfloat16


def lane_iota(shape):
    return lax.broadcasted_iota(jnp.int32, shape, len(shape) - 1)


def row_iota(shape):
    return lax.broadcasted_iota(jnp.int32, shape, 0)


def one_hot(column, width):
    rows = column.shape[0]
    wide = jnp.broadcast_to(column, (rows, LANES)).astype(jnp.int16)
    lanes = lane_iota((rows, LANES))
    one, zero = jnp.ones((rows, LANES), BF16), jnp.zeros((rows, LANES), BF16)
    return jnp.concatenate(
        [
            jnp.where(wide == (lanes + j * LANES).astype(jnp.int16), one, zero)
            for j in range(width // LANES)
        ],
        axis=1,
    )


def silu(x):
    half = 0.5 * x
    return half + half * jnp.tanh(half)


def split(x):
    head = x.astype(BF16).astype(F32)
    return head, x - head


def dot(a, b):
    return jnp.dot(a, b, preferred_element_type=F32)


def choose(both, column):
    number = jnp.broadcast_to(column, (both.shape[0], LANES))
    odd, far = (number & 1) != 0, number >= 2
    parts = [both[:, i * LANES : (i + 1) * LANES] for i in range(4)]
    return jnp.where(far, jnp.where(odd, parts[3], parts[2]), jnp.where(odd, parts[1], parts[0]))


def lane_lookup(rows, hi, lo):
    found = jnp.zeros(lo.shape, F32)
    for r, row in enumerate(rows):
        picked = jnp.take_along_axis(
            jnp.broadcast_to(row, lo.shape), lo, axis=1, mode="promise_in_bounds"
        )
        found = jnp.where(hi == r, picked, found)
    return found


def kernel(
    pos_h, vel_h, spc_h, mas_h, send_h, nbr_h, liv_h, wrad_h, w1_h, w2_h, wup_h, wout_h,
    wts, bns, csr, csr_s,
    opos, ovel, onw,
    pos, vel, spc, mas, send, nbr, liv, wrad, w1, w2, wup, wout,
    send_pos, halo_pos, send_spc, halo_spc, feat, send_feat, halo_feat, filt2, oh, send_oh,
    send_lo, low, gath, disp, ext, waves, wbig, wcat, acc, force, send_frc, recv_frc, every,
    load_sem, send_sem, recv_sem,
):
    n_walk, n_dom = lax.axis_size("walker"), lax.axis_size("domain")
    me_w, me_d = lax.axis_index("walker"), lax.axis_index("domain")
    left = lax.rem(me_d + n_dom - 1, n_dom)
    right = lax.rem(me_d + 1, n_dom)
    walkers, atoms = pos.shape[1], pos.shape[2]
    halo = send.shape[1] // 2
    groups = atoms // LANES
    slots = nbr.shape[1]
    tile_edges = slots * LANES
    peers = [(me_w, left), (me_w, right)]
    ranks = [me_w] + [lax.rem(me_w + o, n_walk) for o in range(1, n_walk)]
    peers += [(rank, me_d) for rank in ranks[1:]]
    peers += [(rank, side) for rank in ranks[1:] for side in (left, right)]

    barrier = pltpu.get_barrier_semaphore()
    for peer in peers:
        pl.semaphore_signal(barrier, inc=1, device_id=peer, device_id_type=MESH)

    loads = {}
    for i, (name, src, dst) in enumerate(
        [
            ("send", send_h, send),
            ("pos", pos_h, pos),
            ("spc", spc_h, spc),
            ("nbr", nbr_h, nbr),
            ("liv", liv_h, liv),
            ("wrad", wrad_h, wrad),
            ("w1", w1_h, w1),
            ("w2", w2_h, w2),
            ("wup", wup_h, wup),
            ("wout", wout_h, wout),
            ("vel", vel_h, vel),
            ("mas", mas_h, mas),
        ]
    ):
        loads[name] = pltpu.make_async_copy(src, dst, load_sem.at[i])
        loads[name].start()

    def remote(src, dst, sem, peer):
        return pltpu.make_async_remote_copy(
            src_ref=src,
            dst_ref=dst,
            send_sem=send_sem.at[sem],
            recv_sem=recv_sem.at[sem],
            device_id=peer,
            device_id_type=MESH,
        )

    def both_ways(src, dst, sem):
        copies = [
            remote(src.at[0], dst.at[1], sem, peers[0]),
            remote(src.at[1], dst.at[0], sem + 1, peers[1]),
        ]
        for copy in copies:
            copy.start()
        return copies

    loads["send"].wait()
    loads["pos"].wait()
    rows_out = jnp.concatenate(
        [send[:, g * LANES : (g + 1) * LANES] for g in range(groups)], axis=0
    )
    out_hi, out_lo = rows_out >> 7, rows_out & (LANES - 1)
    per_side = groups // 2
    for w in range(walkers):
        for c in range(3):
            table = [pos[c, w : w + 1, r * LANES : (r + 1) * LANES] for r in range(groups)]
            sent = lane_lookup(table, out_hi, out_lo)
            row = w * 3 + c
            for g in range(groups):
                q = g % per_side
                send_pos[g // per_side, row : row + 1, q * LANES : (q + 1) * LANES] = sent[g : g + 1]
    quarter = atoms // 4
    columns_out = jnp.transpose(rows_out & (quarter - 1))
    quarters_out = jnp.transpose(rows_out >> 8)
    for g in range(groups):
        block = slice(g * LANES, (g + 1) * LANES)
        hot = one_hot(columns_out[:, g : g + 1], quarter)
        send_oh[block, :] = hot
        send_lo[block, :] = hot[:, :LANES] + hot[:, LANES:]

    def send_gather(rows, target):
        table = jnp.concatenate(
            [rows[i * quarter : (i + 1) * quarter] for i in range(4)], axis=1
        )
        both = dot(send_oh[...], table)
        for g in range(groups):
            picked = choose(both[g * LANES : (g + 1) * LANES], quarters_out[:, g : g + 1])
            q = g % per_side
            target[g // per_side, q * LANES : (q + 1) * LANES, :] = picked.astype(BF16)

    loads["spc"].wait()
    loads["vel"].wait()
    for w in range(walkers):
        for c in range(3):
            every[w, c : c + 1, :] = pos[c, w : w + 1, :]
            every[w, 3 + c : 4 + c, :] = vel[c, w : w + 1, :]
    pl.semaphore_wait(barrier, len(peers))
    moves = both_ways(send_pos, halo_pos, 0)
    send_gather(spc[...], send_spc)
    moves += both_ways(send_spc, halo_spc, 2)
    late_moves = []
    sems = iter(range(4 + 2 * walkers, send_sem.shape[0]))

    def send_late(src, dst, peer):
        copy = remote(src, dst, next(sems), peer)
        copy.start()
        late_moves.append(copy)

    for o in range(1, n_walk):
        mine, theirs = pl.ds(0, walkers), pl.ds(o * walkers, walkers)
        send_late(every.at[mine], every.at[theirs], (ranks[o], me_d))

    for name in ("nbr", "liv", "wrad", "w1", "w2", "wup", "wout", "mas"):
        loads[name].wait()

    def weights_by_slot():
        heads, tails = split(wrad[...])
        sub = row_iota((slots, LANES))
        for s in range(slots):
            blocks = []
            for piece in (heads, tails):
                for _ in range(2):
                    for k in range(piece.shape[0]):
                        line = jnp.broadcast_to(piece[k : k + 1, :], (slots, LANES))
                        blocks.append(jnp.where(sub == s, line, 0.0))
            wbig[:, s * LANES : (s + 1) * LANES] = jnp.concatenate(blocks, axis=0).astype(BF16)

    weights_by_slot()
    wcat[...] = jnp.zeros_like(wcat)
    for i in range(2):
        rows = slice(i * LANES, (i + 1) * LANES)
        wcat[rows, 2 * i * LANES : (2 * i + 1) * LANES] = w1[...]
        wcat[rows, (2 * i + 1) * LANES : (2 * i + 2) * LANES] = w2[...]

    count = wts.shape[1]
    square = (count, count)
    eye = (lane_iota(square) == row_iota(square)).astype(F32)

    def to_column(row):
        return jnp.sum(eye * row, axis=1, keepdims=True)

    def to_row(column):
        return jnp.sum(eye * column, axis=0, keepdims=True)

    w_row, b_row = wts[...], bns[...].astype(F32)
    chosen = (to_column(csr[...].astype(F32)) == lane_iota(square).astype(F32)).astype(F32)
    src_w = jnp.sum(chosen * w_row, axis=1, keepdims=True)
    src_b = jnp.sum(chosen * b_row, axis=1, keepdims=True)
    mass = jnp.sum((src_b == b_row).astype(F32) * w_row, axis=1, keepdims=True)
    share = jnp.sum((src_b == to_row(src_b)).astype(F32) * to_row(src_w), axis=1, keepdims=True)
    onw[...] = to_row(mass * src_w / share)

    def build(w, t):
        at = pl.ds(pl.multiple_of(t * LANES, LANES), LANES)
        ids = nbr[w, :, at]
        key_t = jnp.transpose(jnp.where(liv[w, :, at] != 0, ids & (halo - 1), -1))
        for s in range(slots):
            block = slice(s * LANES, (s + 1) * LANES)
            hot = one_hot(key_t[:, s : s + 1], halo)
            oh[w, t, block, :] = hot
            parts = [hot[:, i * LANES : (i + 1) * LANES] for i in range(halo // LANES)]
            low[w, t, block, :] = functools.reduce(jnp.add, parts)

    def gather_rows(w, t, lane, ids, own, near, part=(0, 8)):
        quarter_t = jnp.transpose(ids >> 9)
        table = jnp.concatenate([own[:halo], own[halo:], near[0], near[1]], axis=1)
        both = dot(oh[w, t, part[0] * LANES : part[1] * LANES, :], table)
        for s in range(*part):
            block = slice(s * LANES, (s + 1) * LANES)
            of = slice((s - part[0]) * LANES, (s - part[0] + 1) * LANES)
            gath[lane, block, :] = choose(both[of], quarter_t[:, s : s + 1])

    def geometry(w, at, ids):
        hi, lo = ids >> 7, ids & (LANES - 1)
        square_sum = None
        for c in range(3):
            table = [ext[w, c, r : r + 1, :] for r in range(2 * groups)]
            delta = lane_lookup(table, hi, lo) - every[w, c : c + 1, at]
            disp[w, c, :, at] = delta
            square_sum = delta * delta if c == 0 else square_sum + delta * delta
        scaled = jnp.sqrt(square_sum) / CUTOFF
        envelope = jnp.square(jnp.maximum(0.0, 1.0 - scaled * scaled))
        first = jnp.cos(jnp.minimum(scaled, 1.0) * math.pi)
        cosines = [first, 2.0 * first * first - 1.0]
        while len(cosines) < wrad.shape[0]:
            cosines.append(2.0 * first * cosines[-1] - cosines[-2])
        pieces = [split(wave * envelope) for wave in cosines]
        stacked = jnp.concatenate([p[0] for p in pieces] + [p[1] for p in pieces], axis=0)
        return jnp.transpose(stacked).astype(BF16)

    def tile_of(number):
        if isinstance(number, int):
            return divmod(number, groups)
        return lax.div(number, groups), lax.rem(number, groups)

    def first_gather(number, lane, part):
        w, t = tile_of(number)
        at = pl.ds(pl.multiple_of(t * LANES, LANES), LANES)
        ids = nbr[w, :, at]
        gather_rows(w, t, lane, ids, spc[...], halo_spc, part)

    def first_waves(number, lane):
        w, t = tile_of(number)
        at = pl.ds(pl.multiple_of(t * LANES, LANES), LANES)
        waves[lane] = geometry(w, at, nbr[w, :, at])

    def first_head(number, lane, ahead, ahead_lane):
        w, t = tile_of(number)
        at = pl.ds(pl.multiple_of(t * LANES, LANES), LANES)
        basis = jnp.concatenate([waves[lane], waves[lane]], axis=1)
        first_waves(ahead, ahead_lane)
        total = jnp.zeros((LANES, LANES), F32)
        for s in range(0, slots, 4):
            hidden = dot(basis, wbig[:, s * LANES : (s + 4) * LANES])
            if CHUNK == 2:
                first_gather(ahead, ahead_lane, (s, s + 2))
            else:
                first_gather(ahead, ahead_lane, (s, s + 4))
            radial = silu(hidden).astype(BF16)
            for i in range(4):
                if i % 2 == 0:
                    pair = dot(radial[:, i * LANES : (i + 2) * LANES], wcat[...])
                    if i == 0 and CHUNK == 2:
                        first_gather(ahead, ahead_lane, (s + 2, s + 4))
                block = slice((s + i) * LANES, (s + i + 1) * LANES)
                column = (i % 2) * 2 * LANES
                filt2[w, t, block, :] = pair[:, column + LANES : column + 2 * LANES]
                total = total + pair[:, column : column + LANES] * gath[lane, block, :]
        updated = dot(total.astype(BF16), wup[...])
        feat[w, at, :] = (spc[at, :].astype(F32) + silu(updated)).astype(BF16)

    def second_gather(w, t, lane):
        at = pl.ds(pl.multiple_of(t * LANES, LANES), LANES)
        ids = nbr[w, :, at]
        gather_rows(w, t, lane, ids, feat[w], halo_feat[w])
        return ids

    def second_head(w, t, lane, ids):
        at = pl.ds(pl.multiple_of(t * LANES, LANES), LANES)
        own = feat[w, at, :].astype(F32) * wout[...]
        lanes = lane_iota((LANES, LANES))
        by_slot = jnp.zeros((LANES, LANES), F32)
        for s in range(slots):
            block = slice(s * LANES, (s + 1) * LANES)
            product = filt2[w, t, block, :] * own * gath[lane, block, :]
            by_slot = jnp.where(lanes == s, jnp.sum(product, axis=1, keepdims=True), by_slot)
        coupling = jnp.transpose(by_slot)[:slots]
        hi = ids >> 7
        pieces = []
        for c in range(3):
            pair = coupling * disp[w, c, :, at]
            force[w, pl.ds(c * groups + t, 1), :] = jnp.sum(pair, axis=0, keepdims=True)
            pieces.append(split(pair))
        acc[...] += dot(spread_left(pieces, hi, 2 * groups), low[w, t])

    def spread_left(pieces, hi, high_count):
        sub = row_iota((high_count, LANES))
        out = []
        for s in range(hi.shape[0]):
            here = jnp.broadcast_to(hi[s : s + 1], (high_count, LANES)) == sub
            rows = [
                jnp.where(here, jnp.broadcast_to(x[p][s : s + 1], (high_count, LANES)), 0.0)
                for p in range(2)
                for x in pieces
            ]
            out.append(jnp.concatenate(rows, axis=0).astype(BF16))
        return jnp.concatenate(out, axis=1)

    def loop(gather, head, w):
        def step(i, carry):
            held = gather(w, i * UNROLL, 0)
            for j in range(UNROLL):
                later = gather(w, i * UNROLL + j + 1, j + 1) if j + 1 < UNROLL else None
                head(w, i * UNROLL + j, j, held)
                held = later
            return carry

        lax.fori_loop(0, groups // UNROLL, step, 0)

    def first_loop(w):
        last = walkers * groups - 1

        def step(i, carry):
            number = w * groups + i * AHEAD
            for j in range(AHEAD):
                ahead = jnp.minimum(number + j + 1, last)
                first_head(number + j, j % 2, ahead, (j + 1) % 2)
            return carry

        lax.fori_loop(0, groups // AHEAD, step, 0)

    def build_all(w):
        def step(i, carry):
            for j in range(2):
                build(w, 2 * i + j)
            return carry

        lax.fori_loop(0, groups // 2, step, 0)

    for w in range(walkers):
        build_all(w)
    for copy in moves:
        copy.wait()
    for w in range(walkers):
        for c in range(3):
            row = w * 3 + c
            for g in range(groups):
                block = slice(g * LANES, (g + 1) * LANES)
                ext[w, c, g : g + 1, :] = pos[c, w : w + 1, block]
                side, q = g // per_side, g % per_side
                shift = 0.0 if c else (OFFSET if side else -OFFSET)
                block = slice(q * LANES, (q + 1) * LANES)
                ext[w, c, groups + g : groups + g + 1, :] = (
                    halo_pos[side, row : row + 1, block] + shift
                )
    first_waves(0, 0)
    first_gather(0, 0, (0, slots))
    feat_moves = []
    for w in range(walkers):
        first_loop(w)
        send_gather(feat[w], send_feat.at[w])
        feat_moves.append(both_ways(send_feat.at[w], halo_feat.at[w], 4 + 2 * w))

    high = 2 * groups
    for w in range(walkers):
        for copy in feat_moves[w]:
            copy.wait()
        acc[...] = jnp.zeros_like(acc)
        loop(second_gather, second_head, w)
        reaction = acc[: 3 * high] + acc[3 * high :]
        for c in range(3):
            for side in range(2):
                start = c * high + groups + side * per_side
                send_frc[w, side, c * per_side : (c + 1) * per_side, :] = -reaction[
                    start : start + per_side
                ]
            force[w, c * groups : (c + 1) * groups, :] = (
                force[w, c * groups : (c + 1) * groups, :] - reaction[c * high : c * high + groups]
            )
        for o in range(n_walk):
            slot = o * walkers + w
            send_late(send_frc.at[w, 0], recv_frc.at[slot, 1], (ranks[o], left))
            send_late(send_frc.at[w, 1], recv_frc.at[slot, 0], (ranks[o], right))
            if o:
                send_late(force.at[w], force.at[slot], (ranks[o], me_d))
    for copy in late_moves:
        copy.wait()
    for k in range(walkers):
        source = csr_s[me_w * walkers + k]
        behind = lax.rem(me_w - lax.div(source, walkers) + n_walk, n_walk)
        slot = behind * walkers + lax.rem(source, walkers)
        state, own, back = every[slot], force[slot], recv_frc[slot]
        pieces = []
        for c in range(3):
            rows = slice(c * per_side, (c + 1) * per_side)
            pieces.append(split(jnp.concatenate([back[0, rows], back[1, rows]], axis=0)))
        spread_back = dot(spread_left(pieces, out_hi, groups), send_lo[...])
        for c in range(3):
            total = own[c * groups : (c + 1) * groups] + (
                spread_back[c * groups : (c + 1) * groups]
                + spread_back[(3 + c) * groups : (4 + c) * groups]
            )
            flat = jnp.concatenate([total[g : g + 1] for g in range(groups)], axis=1)
            stepped = state[3 + c : 4 + c] + STEP * flat / mas[...]
            opos[c, k : k + 1, :] = state[c : c + 1] + STEP * stepped
            ovel[c, k : k + 1, :] = stepped


def on_device(
    positions,
    velocities,
    species,
    masses,
    send_rows,
    neighbours,
    live_edges,
    w_rad,
    w_first,
    w_second,
    w_update,
    w_out,
    weights,
    bins,
    copy_src,
):
    walkers, _, atoms = positions.shape
    channels = species.shape[1]
    halo = send_rows.shape[0] // 2
    groups = atoms // LANES
    slots = neighbours.shape[1]
    orders = w_rad.shape[0]
    n_walk = lax.axis_size("walker")
    edges = slots * LANES
    copies = 4 + 2 * walkers + (n_walk - 1) + walkers * (3 * n_walk - 1)
    by_component = (3, walkers, atoms)
    hbm = pl.BlockSpec(memory_space=pltpu.HBM)
    vmem = pl.BlockSpec(memory_space=pltpu.VMEM)
    smem = pl.BlockSpec(memory_space=pltpu.SMEM)
    halo_rows = (2, halo, channels)
    out_positions, out_velocities, new_weights = pl.pallas_call(
        kernel,
        out_shape=(
            jax.ShapeDtypeStruct(by_component, F32),
            jax.ShapeDtypeStruct(by_component, F32),
            jax.ShapeDtypeStruct((1, weights.shape[0]), F32),
        ),
        in_specs=[hbm] * 12 + [vmem] * 3 + [smem],
        out_specs=(vmem, vmem, vmem),
        scratch_shapes=[
            pltpu.VMEM(by_component, F32),
            pltpu.VMEM(by_component, F32),
            pltpu.VMEM(species.shape, BF16),
            pltpu.VMEM((1, atoms), F32),
            pltpu.VMEM((1, 2 * halo), jnp.int32),
            pltpu.VMEM(neighbours.shape, jnp.int32),
            pltpu.VMEM(live_edges.shape, jnp.int32),
            pltpu.VMEM(w_rad.shape, F32),
            pltpu.VMEM(w_first.shape, BF16),
            pltpu.VMEM(w_second.shape, BF16),
            pltpu.VMEM(w_update.shape, BF16),
            pltpu.VMEM((1, channels), F32),
            pltpu.VMEM((2, 8, halo), F32),
            pltpu.VMEM((2, 8, halo), F32),
            pltpu.VMEM(halo_rows, BF16),
            pltpu.VMEM(halo_rows, BF16),
            pltpu.VMEM((walkers, atoms, channels), BF16),
            pltpu.VMEM((walkers, *halo_rows), BF16),
            pltpu.VMEM((walkers, *halo_rows), BF16),
            pltpu.VMEM((walkers, groups, edges, channels), F32),
            pltpu.VMEM((walkers, groups, edges, halo), BF16),
            pltpu.VMEM((2 * halo, atoms // 4), BF16),
            pltpu.VMEM((2 * halo, LANES), BF16),
            pltpu.VMEM((walkers, groups, edges, LANES), BF16),
            pltpu.VMEM((UNROLL, edges, channels), F32),
            pltpu.VMEM((walkers, 3, slots, atoms), F32),
            pltpu.VMEM((walkers, 3, 2 * groups, LANES), F32),
            pltpu.VMEM((2, LANES, 2 * orders * slots), BF16),
            pltpu.VMEM((4 * orders * slots, slots * channels), BF16),
            pltpu.VMEM((2 * channels, 4 * channels), BF16),
            pltpu.VMEM((12 * groups, LANES), F32),
            pltpu.VMEM((n_walk * walkers, 3 * groups, LANES), F32),
            pltpu.VMEM((walkers, 2, 16, LANES), F32),
            pltpu.VMEM((n_walk * walkers, 2, 16, LANES), F32),
            pltpu.VMEM((n_walk * walkers, 8, atoms), F32),
            pltpu.SemaphoreType.DMA((12,)),
            pltpu.SemaphoreType.DMA((copies,)),
            pltpu.SemaphoreType.DMA((copies,)),
        ],
        compiler_params=pltpu.CompilerParams(
            collective_id=0, has_side_effects=True, vmem_limit_bytes=58 * 2**20
        ),
    )(
        jnp.transpose(positions, (1, 0, 2)),
        jnp.transpose(velocities, (1, 0, 2)),
        species,
        masses[None],
        send_rows[None],
        neighbours,
        live_edges,
        w_rad,
        w_first,
        w_second,
        w_update,
        w_out[None],
        weights[None],
        bins[None],
        copy_src[None],
        copy_src,
    )
    return (
        jnp.transpose(out_positions, (1, 0, 2)),
        jnp.transpose(out_velocities, (1, 0, 2)),
        new_weights[0],
    )


def solution(mesh):
    in_specs = (
        P("walker", None, "domain"),
        P("walker", None, "domain"),
        P("domain", None),
        P("domain"),
        P("domain"),
        P("walker", None, "domain"),
        P("walker", None, "domain"),
        P(),
        P(),
        P(),
        P(),
        P(),
        P(),
        P(),
        P(),
    )
    out_specs = (P("walker", None, "domain"), P("walker", None, "domain"), P())
    return jax.shard_map(
        on_device, mesh=mesh, in_specs=in_specs, out_specs=out_specs, check_vma=False
    )
```

```python
import functools
import math

import jax
import jax.numpy as jnp
from jax import lax
from jax.experimental import pallas as pl
from jax.experimental.pallas import tpu as pltpu
from jax.sharding import PartitionSpec as P

OFFSET = 2.0
CUTOFF = 5.0
STEP = 0.2
LANES = 128
UNROLL = 8
AHEAD = 2
MESH = pl.DeviceIdType.MESH
F32 = jnp.float32
BF16 = jnp.bfloat16


def lane_iota(shape):
    return lax.broadcasted_iota(jnp.int32, shape, len(shape) - 1)


def row_iota(shape):
    return lax.broadcasted_iota(jnp.int32, shape, 0)


def one_hot(column, width):
    rows = column.shape[0]
    wide = jnp.broadcast_to(column, (rows, LANES)).astype(jnp.int16)
    lanes = lane_iota((rows, LANES))
    one, zero = jnp.ones((rows, LANES), BF16), jnp.zeros((rows, LANES), BF16)
    return jnp.concatenate(
        [
            jnp.where(wide == (lanes + j * LANES).astype(jnp.int16), one, zero)
            for j in range(width // LANES)
        ],
        axis=1,
    )


def silu(x):
    half = 0.5 * x
    return half + half * jnp.tanh(half)


def split(x):
    head = x.astype(BF16).astype(F32)
    return head, x - head


def dot(a, b):
    return jnp.dot(a, b, preferred_element_type=F32)


def choose(both, column):
    number = jnp.broadcast_to(column, (both.shape[0], LANES))
    odd, far = (number & 1) != 0, number >= 2
    parts = [both[:, i * LANES : (i + 1) * LANES] for i in range(4)]
    return jnp.where(far, jnp.where(odd, parts[3], parts[2]), jnp.where(odd, parts[1], parts[0]))


def lane_lookup(rows, hi, lo):
    found = jnp.zeros(lo.shape, F32)
    for r, row in enumerate(rows):
        picked = jnp.take_along_axis(
            jnp.broadcast_to(row, lo.shape), lo, axis=1, mode="promise_in_bounds"
        )
        found = jnp.where(hi == r, picked, found)
    return found


def kernel(
    pos_h, vel_h, spc_h, mas_h, send_h, nbr_h, liv_h, wrad_h, w1_h, w2_h, wup_h, wout_h,
    wts, bns, csr, csr_s,
    opos, ovel, onw,
    pos, vel, spc, mas, send, nbr, liv, wrad, w1, w2, wup, wout,
    send_pos, halo_pos, send_spc, halo_spc, feat, send_feat, halo_feat, filt2, oh, send_oh,
    send_lo, low, gath, disp, ext, waves, wbig, wcat, acc, force, send_frc, recv_frc, every,
    load_sem, send_sem, recv_sem,
):
    n_walk, n_dom = lax.axis_size("walker"), lax.axis_size("domain")
    me_w, me_d = lax.axis_index("walker"), lax.axis_index("domain")
    left = lax.rem(me_d + n_dom - 1, n_dom)
    right = lax.rem(me_d + 1, n_dom)
    walkers, atoms = pos.shape[1], pos.shape[2]
    halo = send.shape[1] // 2
    groups = atoms // LANES
    slots = nbr.shape[1]
    tile_edges = slots * LANES
    peers = [(me_w, left), (me_w, right)]
    ranks = [me_w] + [lax.rem(me_w + o, n_walk) for o in range(1, n_walk)]
    peers += [(rank, me_d) for rank in ranks[1:]]
    peers += [(rank, side) for rank in ranks[1:] for side in (left, right)]

    barrier = pltpu.get_barrier_semaphore()
    for peer in peers:
        pl.semaphore_signal(barrier, inc=1, device_id=peer, device_id_type=MESH)

    loads = {}
    for i, (name, src, dst) in enumerate(
        [
            ("send", send_h, send),
            ("pos", pos_h, pos),
            ("spc", spc_h, spc),
            ("nbr", nbr_h, nbr),
            ("liv", liv_h, liv),
            ("wrad", wrad_h, wrad),
            ("w1", w1_h, w1),
            ("w2", w2_h, w2),
            ("wup", wup_h, wup),
            ("wout", wout_h, wout),
            ("vel", vel_h, vel),
            ("mas", mas_h, mas),
        ]
    ):
        loads[name] = pltpu.make_async_copy(src, dst, load_sem.at[i])
        loads[name].start()

    def remote(src, dst, sem, peer):
        return pltpu.make_async_remote_copy(
            src_ref=src,
            dst_ref=dst,
            send_sem=send_sem.at[sem],
            recv_sem=recv_sem.at[sem],
            device_id=peer,
            device_id_type=MESH,
        )

    def both_ways(src, dst, sem):
        copies = [
            remote(src.at[0], dst.at[1], sem, peers[0]),
            remote(src.at[1], dst.at[0], sem + 1, peers[1]),
        ]
        for copy in copies:
            copy.start()
        return copies

    loads["send"].wait()
    loads["pos"].wait()
    rows_out = jnp.concatenate(
        [send[:, g * LANES : (g + 1) * LANES] for g in range(groups)], axis=0
    )
    out_hi, out_lo = rows_out >> 7, rows_out & (LANES - 1)
    per_side = groups // 2
    for w in range(walkers):
        for c in range(3):
            table = [pos[c, w : w + 1, r * LANES : (r + 1) * LANES] for r in range(groups)]
            sent = lane_lookup(table, out_hi, out_lo)
            row = w * 3 + c
            for g in range(groups):
                q = g % per_side
                send_pos[g // per_side, row : row + 1, q * LANES : (q + 1) * LANES] = sent[g : g + 1]
    quarter = atoms // 4
    columns_out = jnp.transpose(rows_out & (quarter - 1))
    quarters_out = jnp.transpose(rows_out >> 8)
    for g in range(groups):
        block = slice(g * LANES, (g + 1) * LANES)
        hot = one_hot(columns_out[:, g : g + 1], quarter)
        send_oh[block, :] = hot
        send_lo[block, :] = hot[:, :LANES] + hot[:, LANES:]

    def send_gather(rows, target):
        table = jnp.concatenate(
            [rows[i * quarter : (i + 1) * quarter] for i in range(4)], axis=1
        )
        both = dot(send_oh[...], table)
        for g in range(groups):
            picked = choose(both[g * LANES : (g + 1) * LANES], quarters_out[:, g : g + 1])
            q = g % per_side
            target[g // per_side, q * LANES : (q + 1) * LANES, :] = picked.astype(BF16)

    loads["spc"].wait()
    loads["vel"].wait()
    for w in range(walkers):
        for c in range(3):
            every[w, c : c + 1, :] = pos[c, w : w + 1, :]
            every[w, 3 + c : 4 + c, :] = vel[c, w : w + 1, :]
    pl.semaphore_wait(barrier, len(peers))
    moves = both_ways(send_pos, halo_pos, 0)
    send_gather(spc[...], send_spc)
    moves += both_ways(send_spc, halo_spc, 2)
    late_moves = []
    sems = iter(range(4 + 2 * walkers, send_sem.shape[0]))

    def send_late(src, dst, peer):
        copy = remote(src, dst, next(sems), peer)
        copy.start()
        late_moves.append(copy)

    for o in range(1, n_walk):
        mine, theirs = pl.ds(0, walkers), pl.ds(o * walkers, walkers)
        send_late(every.at[mine], every.at[theirs], (ranks[o], me_d))

    for name in ("nbr", "liv", "wrad", "w1", "w2", "wup", "wout", "mas"):
        loads[name].wait()

    def weights_by_slot():
        heads, tails = split(wrad[...])
        sub = row_iota((slots, LANES))
        for s in range(slots):
            blocks = []
            for piece in (heads, tails):
                for _ in range(2):
                    for k in range(piece.shape[0]):
                        line = jnp.broadcast_to(piece[k : k + 1, :], (slots, LANES))
                        blocks.append(jnp.where(sub == s, line, 0.0))
            wbig[:, s * LANES : (s + 1) * LANES] = jnp.concatenate(blocks, axis=0).astype(BF16)

    weights_by_slot()
    wcat[...] = jnp.zeros_like(wcat)
    for i in range(2):
        rows = slice(i * LANES, (i + 1) * LANES)
        wcat[rows, 2 * i * LANES : (2 * i + 1) * LANES] = w1[...]
        wcat[rows, (2 * i + 1) * LANES : (2 * i + 2) * LANES] = w2[...]

    count = wts.shape[1]
    square = (count, count)
    eye = (lane_iota(square) == row_iota(square)).astype(F32)

    def to_column(row):
        return jnp.sum(eye * row, axis=1, keepdims=True)

    def to_row(column):
        return jnp.sum(eye * column, axis=0, keepdims=True)

    w_row, b_row = wts[...], bns[...].astype(F32)
    chosen = (to_column(csr[...].astype(F32)) == lane_iota(square).astype(F32)).astype(F32)
    src_w = jnp.sum(chosen * w_row, axis=1, keepdims=True)
    src_b = jnp.sum(chosen * b_row, axis=1, keepdims=True)
    mass = jnp.sum((src_b == b_row).astype(F32) * w_row, axis=1, keepdims=True)
    share = jnp.sum((src_b == to_row(src_b)).astype(F32) * to_row(src_w), axis=1, keepdims=True)
    onw[...] = to_row(mass * src_w / share)

    def build(w, t):
        at = pl.ds(pl.multiple_of(t * LANES, LANES), LANES)
        ids = nbr[w, :, at]
        key_t = jnp.transpose(jnp.where(liv[w, :, at] != 0, ids & (halo - 1), -1))
        for s in range(slots):
            block = slice(s * LANES, (s + 1) * LANES)
            hot = one_hot(key_t[:, s : s + 1], halo)
            oh[w, t, block, :] = hot
            parts = [hot[:, i * LANES : (i + 1) * LANES] for i in range(halo // LANES)]
            low[w, t, block, :] = functools.reduce(jnp.add, parts)

    def gather_rows(w, t, lane, ids, own, near, part=(0, 8)):
        quarter_t = jnp.transpose(ids >> 9)
        table = jnp.concatenate([own[:halo], own[halo:], near[0], near[1]], axis=1)
        both = dot(oh[w, t, part[0] * LANES : part[1] * LANES, :], table)
        for s in range(*part):
            block = slice(s * LANES, (s + 1) * LANES)
            of = slice((s - part[0]) * LANES, (s - part[0] + 1) * LANES)
            gath[lane, block, :] = choose(both[of], quarter_t[:, s : s + 1])

    def geometry(w, at, ids):
        hi, lo = ids >> 7, ids & (LANES - 1)
        square_sum = None
        for c in range(3):
            table = [ext[w, c, r : r + 1, :] for r in range(2 * groups)]
            delta = lane_lookup(table, hi, lo) - every[w, c : c + 1, at]
            disp[w, c, :, at] = delta
            square_sum = delta * delta if c == 0 else square_sum + delta * delta
        scaled = jnp.sqrt(square_sum) / CUTOFF
        envelope = jnp.square(jnp.maximum(0.0, 1.0 - scaled * scaled))
        first = jnp.cos(jnp.minimum(scaled, 1.0) * math.pi)
        cosines = [first, 2.0 * first * first - 1.0]
        while len(cosines) < wrad.shape[0]:
            cosines.append(2.0 * first * cosines[-1] - cosines[-2])
        pieces = [split(wave * envelope) for wave in cosines]
        stacked = jnp.concatenate([p[0] for p in pieces] + [p[1] for p in pieces], axis=0)
        return jnp.transpose(stacked).astype(BF16)

    def tile_of(number):
        if isinstance(number, int):
            return divmod(number, groups)
        return lax.div(number, groups), lax.rem(number, groups)

    def first_gather(number, lane, part):
        w, t = tile_of(number)
        at = pl.ds(pl.multiple_of(t * LANES, LANES), LANES)
        ids = nbr[w, :, at]
        gather_rows(w, t, lane, ids, spc[...], halo_spc, part)

    def first_waves(number, lane):
        w, t = tile_of(number)
        at = pl.ds(pl.multiple_of(t * LANES, LANES), LANES)
        waves[lane] = geometry(w, at, nbr[w, :, at])

    def first_head(number, lane, ahead, ahead_lane):
        w, t = tile_of(number)
        at = pl.ds(pl.multiple_of(t * LANES, LANES), LANES)
        basis = jnp.concatenate([waves[lane], waves[lane]], axis=1)
        first_waves(ahead, ahead_lane)
        total = jnp.zeros((LANES, LANES), F32)
        for s in range(0, slots, 4):
            hidden = dot(basis, wbig[:, s * LANES : (s + 4) * LANES])
            first_gather(ahead, ahead_lane, (0, 3) if s == 0 else (3, 6))
            radial = silu(hidden).astype(BF16)
            for i in range(4):
                if i % 2 == 0:
                    pair = dot(radial[:, i * LANES : (i + 2) * LANES], wcat[...])
                block = slice((s + i) * LANES, (s + i + 1) * LANES)
                column = (i % 2) * 2 * LANES
                filt2[w, t, block, :] = pair[:, column + LANES : column + 2 * LANES]
                total = total + pair[:, column : column + LANES] * gath[lane, block, :]
        first_gather(ahead, ahead_lane, (6, slots))
        updated = dot(total.astype(BF16), wup[...])
        feat[w, at, :] = (spc[at, :].astype(F32) + silu(updated)).astype(BF16)

    def second_gather(w, t, lane):
        at = pl.ds(pl.multiple_of(t * LANES, LANES), LANES)
        ids = nbr[w, :, at]
        gather_rows(w, t, lane, ids, feat[w], halo_feat[w])
        return ids

    def second_head(w, t, lane, ids):
        at = pl.ds(pl.multiple_of(t * LANES, LANES), LANES)
        own = feat[w, at, :].astype(F32) * wout[...]
        lanes = lane_iota((LANES, LANES))
        by_slot = jnp.zeros((LANES, LANES), F32)
        for s in range(slots):
            block = slice(s * LANES, (s + 1) * LANES)
            product = filt2[w, t, block, :] * own * gath[lane, block, :]
            by_slot = jnp.where(lanes == s, jnp.sum(product, axis=1, keepdims=True), by_slot)
        coupling = jnp.transpose(by_slot)[:slots]
        hi = ids >> 7
        pieces = []
        for c in range(3):
            pair = coupling * disp[w, c, :, at]
            force[w, pl.ds(c * groups + t, 1), :] = jnp.sum(pair, axis=0, keepdims=True)
            pieces.append(split(pair))
        acc[...] += dot(spread_left(pieces, hi, 2 * groups), low[w, t])

    def spread_left(pieces, hi, high_count):
        sub = row_iota((high_count, LANES))
        out = []
        for s in range(hi.shape[0]):
            here = jnp.broadcast_to(hi[s : s + 1], (high_count, LANES)) == sub
            rows = [
                jnp.where(here, jnp.broadcast_to(x[p][s : s + 1], (high_count, LANES)), 0.0)
                for p in range(2)
                for x in pieces
            ]
            out.append(jnp.concatenate(rows, axis=0).astype(BF16))
        return jnp.concatenate(out, axis=1)

    def loop(gather, head, w):
        def step(i, carry):
            held = gather(w, i * UNROLL, 0)
            for j in range(UNROLL):
                later = gather(w, i * UNROLL + j + 1, j + 1) if j + 1 < UNROLL else None
                head(w, i * UNROLL + j, j, held)
                held = later
            return carry

        lax.fori_loop(0, groups // UNROLL, step, 0)

    def first_loop(w):
        last = walkers * groups - 1

        def step(i, carry):
            number = w * groups + i * AHEAD
            for j in range(AHEAD):
                ahead = jnp.minimum(number + j + 1, last)
                first_head(number + j, j % 2, ahead, (j + 1) % 2)
            return carry

        lax.fori_loop(0, groups // AHEAD, step, 0)

    def build_all(w):
        def step(i, carry):
            for j in range(2):
                build(w, 2 * i + j)
            return carry

        lax.fori_loop(0, groups // 2, step, 0)

    for w in range(walkers):
        build_all(w)
    for copy in moves:
        copy.wait()
    for w in range(walkers):
        for c in range(3):
            row = w * 3 + c
            for g in range(groups):
                block = slice(g * LANES, (g + 1) * LANES)
                ext[w, c, g : g + 1, :] = pos[c, w : w + 1, block]
                side, q = g // per_side, g % per_side
                shift = 0.0 if c else (OFFSET if side else -OFFSET)
                block = slice(q * LANES, (q + 1) * LANES)
                ext[w, c, groups + g : groups + g + 1, :] = (
                    halo_pos[side, row : row + 1, block] + shift
                )
    first_waves(0, 0)
    first_gather(0, 0, (0, slots))
    feat_moves = []
    for w in range(walkers):
        first_loop(w)
        send_gather(feat[w], send_feat.at[w])
        feat_moves.append(both_ways(send_feat.at[w], halo_feat.at[w], 4 + 2 * w))

    high = 2 * groups
    for w in range(walkers):
        for copy in feat_moves[w]:
            copy.wait()
        acc[...] = jnp.zeros_like(acc)
        loop(second_gather, second_head, w)
        reaction = acc[: 3 * high] + acc[3 * high :]
        for c in range(3):
            for side in range(2):
                start = c * high + groups + side * per_side
                send_frc[w, side, c * per_side : (c + 1) * per_side, :] = -reaction[
                    start : start + per_side
                ]
            force[w, c * groups : (c + 1) * groups, :] = (
                force[w, c * groups : (c + 1) * groups, :] - reaction[c * high : c * high + groups]
            )
        for o in range(n_walk):
            slot = o * walkers + w
            send_late(send_frc.at[w, 0], recv_frc.at[slot, 1], (ranks[o], left))
            send_late(send_frc.at[w, 1], recv_frc.at[slot, 0], (ranks[o], right))
            if o:
                send_late(force.at[w], force.at[slot], (ranks[o], me_d))
    for copy in late_moves:
        copy.wait()
    for k in range(walkers):
        source = csr_s[me_w * walkers + k]
        behind = lax.rem(me_w - lax.div(source, walkers) + n_walk, n_walk)
        slot = behind * walkers + lax.rem(source, walkers)
        state, own, back = every[slot], force[slot], recv_frc[slot]
        pieces = []
        for c in range(3):
            rows = slice(c * per_side, (c + 1) * per_side)
            pieces.append(split(jnp.concatenate([back[0, rows], back[1, rows]], axis=0)))
        spread_back = dot(spread_left(pieces, out_hi, groups), send_lo[...])
        for c in range(3):
            total = own[c * groups : (c + 1) * groups] + (
                spread_back[c * groups : (c + 1) * groups]
                + spread_back[(3 + c) * groups : (4 + c) * groups]
            )
            flat = jnp.concatenate([total[g : g + 1] for g in range(groups)], axis=1)
            stepped = state[3 + c : 4 + c] + STEP * flat / mas[...]
            opos[c, k : k + 1, :] = state[c : c + 1] + STEP * stepped
            ovel[c, k : k + 1, :] = stepped


def on_device(
    positions,
    velocities,
    species,
    masses,
    send_rows,
    neighbours,
    live_edges,
    w_rad,
    w_first,
    w_second,
    w_update,
    w_out,
    weights,
    bins,
    copy_src,
):
    walkers, _, atoms = positions.shape
    channels = species.shape[1]
    halo = send_rows.shape[0] // 2
    groups = atoms // LANES
    slots = neighbours.shape[1]
    orders = w_rad.shape[0]
    n_walk = lax.axis_size("walker")
    edges = slots * LANES
    copies = 4 + 2 * walkers + (n_walk - 1) + walkers * (3 * n_walk - 1)
    by_component = (3, walkers, atoms)
    hbm = pl.BlockSpec(memory_space=pltpu.HBM)
    vmem = pl.BlockSpec(memory_space=pltpu.VMEM)
    smem = pl.BlockSpec(memory_space=pltpu.SMEM)
    halo_rows = (2, halo, channels)
    out_positions, out_velocities, new_weights = pl.pallas_call(
        kernel,
        out_shape=(
            jax.ShapeDtypeStruct(by_component, F32),
            jax.ShapeDtypeStruct(by_component, F32),
            jax.ShapeDtypeStruct((1, weights.shape[0]), F32),
        ),
        in_specs=[hbm] * 12 + [vmem] * 3 + [smem],
        out_specs=(vmem, vmem, vmem),
        scratch_shapes=[
            pltpu.VMEM(by_component, F32),
            pltpu.VMEM(by_component, F32),
            pltpu.VMEM(species.shape, BF16),
            pltpu.VMEM((1, atoms), F32),
            pltpu.VMEM((1, 2 * halo), jnp.int32),
            pltpu.VMEM(neighbours.shape, jnp.int32),
            pltpu.VMEM(live_edges.shape, jnp.int32),
            pltpu.VMEM(w_rad.shape, F32),
            pltpu.VMEM(w_first.shape, BF16),
            pltpu.VMEM(w_second.shape, BF16),
            pltpu.VMEM(w_update.shape, BF16),
            pltpu.VMEM((1, channels), F32),
            pltpu.VMEM((2, 8, halo), F32),
            pltpu.VMEM((2, 8, halo), F32),
            pltpu.VMEM(halo_rows, BF16),
            pltpu.VMEM(halo_rows, BF16),
            pltpu.VMEM((walkers, atoms, channels), BF16),
            pltpu.VMEM((walkers, *halo_rows), BF16),
            pltpu.VMEM((walkers, *halo_rows), BF16),
            pltpu.VMEM((walkers, groups, edges, channels), F32),
            pltpu.VMEM((walkers, groups, edges, halo), BF16),
            pltpu.VMEM((2 * halo, atoms // 4), BF16),
            pltpu.VMEM((2 * halo, LANES), BF16),
            pltpu.VMEM((walkers, groups, edges, LANES), BF16),
            pltpu.VMEM((UNROLL, edges, channels), F32),
            pltpu.VMEM((walkers, 3, slots, atoms), F32),
            pltpu.VMEM((walkers, 3, 2 * groups, LANES), F32),
            pltpu.VMEM((2, LANES, 2 * orders * slots), BF16),
            pltpu.VMEM((4 * orders * slots, slots * channels), BF16),
            pltpu.VMEM((2 * channels, 4 * channels), BF16),
            pltpu.VMEM((12 * groups, LANES), F32),
            pltpu.VMEM((n_walk * walkers, 3 * groups, LANES), F32),
            pltpu.VMEM((walkers, 2, 16, LANES), F32),
            pltpu.VMEM((n_walk * walkers, 2, 16, LANES), F32),
            pltpu.VMEM((n_walk * walkers, 8, atoms), F32),
            pltpu.SemaphoreType.DMA((12,)),
            pltpu.SemaphoreType.DMA((copies,)),
            pltpu.SemaphoreType.DMA((copies,)),
        ],
        compiler_params=pltpu.CompilerParams(
            collective_id=0, has_side_effects=True, vmem_limit_bytes=58 * 2**20
        ),
    )(
        jnp.transpose(positions, (1, 0, 2)),
        jnp.transpose(velocities, (1, 0, 2)),
        species,
        masses[None],
        send_rows[None],
        neighbours,
        live_edges,
        w_rad,
        w_first,
        w_second,
        w_update,
        w_out[None],
        weights[None],
        bins[None],
        copy_src[None],
        copy_src,
    )
    return (
        jnp.transpose(out_positions, (1, 0, 2)),
        jnp.transpose(out_velocities, (1, 0, 2)),
        new_weights[0],
    )


def solution(mesh):
    in_specs = (
        P("walker", None, "domain"),
        P("walker", None, "domain"),
        P("domain", None),
        P("domain"),
        P("domain"),
        P("walker", None, "domain"),
        P("walker", None, "domain"),
        P(),
        P(),
        P(),
        P(),
        P(),
        P(),
        P(),
        P(),
    )
    out_specs = (P("walker", None, "domain"), P("walker", None, "domain"), P())
    return jax.shard_map(
        on_device, mesh=mesh, in_specs=in_specs, out_specs=out_specs, check_vma=False
    )
```
